32 devices in a mesh: clip: 2 (over core), tm: 16 (over z, y, x).
Axes of the slice: x: 2, y: 2, z: 4, core: 2. Of those that a mesh axis runs over, the one named last changes fastest.
Arguments:
- clip_frames: bfloat16 [2, 32, 64, 64, 128], P('clip', 'tm'), may hold values from -6 to 6
- spatial_weight: bfloat16 [3, 3, 128, 256], replicated, may hold values from -0.1875 to 0.1875
- norm_gain: float32 [256], replicated, may hold values from 0.5 to 1.5
- norm_bias: float32 [256], replicated, may hold values from -3 to 3
- temporal_weight: bfloat16 [3, 256, 256], replicated, may hold values from -0.21875 to 0.21875
- cotangent: bfloat16 [2, 32, 32, 32, 256], P('clip', 'tm'), may hold values from -0.0234375 to 0.0234375
Outputs:
- mixed: bfloat16 [2, 32, 32, 32, 256], P('clip', 'tm')
- spatial_grad: float32 [3, 3, 128, 256], replicated
- gain_grad: float32 [256], replicated
- bias_grad: float32 [256], replicated
- temporal_grad: float32 [3, 256, 256], replicated
The draws below stay inside these ranges and needn't reach their ends.
All inputs are finite; a program needn't handle non-finite values.
Results may differ from the reference program's by a relative error of at most 0.0085.
Values may be sent and summed in bfloat16 or wider, within the bound.
A program may use at most 64 MiB of HBM per device.

```python
import jax
import jax.numpy as jnp
from jax import lax

C1 = 128
C2 = 256
GROUPS = 32
DILATION_FRAMES = 4
HEIGHT = 64
WIDTH = 64
CLIPS = 2
FRAMES = 32
H2 = 32
W2 = 32


def block_scale(key, extent, shards, low, top_value):
    factor_of = 1.0
    for position, shards_of in shards:
        heights = jax.random.uniform(jax.random.fold_in(jax.random.fold_in(key, 6), position), (shards_of,), jnp.float32, low / len(shards), top_value / len(shards))
        factor_of = factor_of * jnp.repeat(jnp.exp(heights), extent[position] // shards_of).reshape((-1,) + (1,) * (len(extent) - 1 - position))
    return factor_of


def scatter_about(stream_key, extent, scale, reach, cuts=(), kind=jnp.bfloat16):
    loudness = block_scale(stream_key, extent, cuts, -0.22, 0.18) if cuts else 1.0
    values = jax.random.normal(stream_key, extent, jnp.float32) * scale * loudness
    return jnp.minimum(jnp.maximum(values, -reach), reach).astype(kind)


def setup_inputs(seed: int = 0) -> dict:
    streams_of = jax.random.split(jax.random.key(seed), 7)
    return {
        "clip_frames": scatter_about(streams_of[0], (CLIPS, FRAMES, HEIGHT, WIDTH, C1), 1.0, 6.0, ((0, 2), (1, 16))),
        "spatial_weight": scatter_about(streams_of[1], (3, 3, C1, C2), (9 * C1) ** -0.5, 0.1875),
        "norm_gain": jnp.clip(1.0 + 0.1 * jax.random.normal(streams_of[2], (C2,), jnp.float32), 0.5, 1.5),
        "norm_bias": scatter_about(streams_of[3], (C2,), 0.5, 3.0, (), jnp.float32),
        "temporal_weight": scatter_about(streams_of[4], (3, C2, C2), (3 * C2) ** -0.5, 0.21875),
        "cotangent": scatter_about(streams_of[5], (CLIPS, FRAMES, H2, W2, C2), (1.0 / (CLIPS * FRAMES * H2 * W2) ** 0.5), 0.0234375, ((0, 2), (1, 16))),
    }


epsilon = 1e-05

def gather_patches(frames_in):
    height = frames_in.shape[1]
    width = frames_in.shape[2]
    padded = jnp.pad(frames_in, ((0, 0), (1, 1), (1, 1), (0, 0)))
    pieces = []
    for row_offset in range(3):
        for col_offset in range(3):
            pieces.append(padded[:, row_offset:row_offset + height:2, col_offset:col_offset + width:2, :])
    return jnp.concatenate(pieces, axis=-1)

def activate(conv_out, gain, bias):
    grouped = conv_out.reshape(conv_out.shape[:-1] + (GROUPS, conv_out.shape[-1] // GROUPS))
    center = lax.optimization_barrier(jnp.mean(grouped, axis=(1, 2, 4), keepdims=True))
    temporal_reach = lax.optimization_barrier(jnp.mean((grouped - center) ** 2, axis=(1, 2, 4), keepdims=True))
    normed = ((grouped - center) * lax.rsqrt(temporal_reach + epsilon)).reshape(conv_out.shape)
    return jax.nn.silu(normed * gain + bias)

def padded_lag(values, frame_offset):
    if frame_offset == 0:
        return values
    frames = values.shape[0]
    if frame_offset > 0:
        filler = jnp.zeros((frame_offset,) + values.shape[1:], values.dtype)
        return jnp.concatenate([filler, values[:frames - frame_offset]], axis=0)
    filler = jnp.zeros((-frame_offset,) + values.shape[1:], values.dtype)
    return jnp.concatenate([values[-frame_offset:], filler], axis=0)

def temporal_pass(acts, grads, weight):
    chans = acts.shape[-1]
    total = acts.astype(jnp.float32)
    backward_total_sum = grads.astype(jnp.float32)
    tap_grads = []
    flattened_gradients = grads.reshape(-1, chans)
    for kernel_tap_index in range(3):
        frame_offset = kernel_tap_index * DILATION_FRAMES
        earlier = padded_lag(acts, frame_offset).reshape(-1, chans)
        later = padded_lag(grads, -frame_offset).reshape(-1, chans)
        total = total + jnp.dot(earlier, weight[kernel_tap_index], preferred_element_type=jnp.float32).reshape(acts.shape)
        backward_total_sum = backward_total_sum + jnp.dot(later, weight[kernel_tap_index].T, preferred_element_type=jnp.float32).reshape(acts.shape)
        tap_grads.append(lax.dot_general(earlier, flattened_gradients, (((0,), (0,)), ((), ())), preferred_element_type=jnp.float32))
    return (total.astype(jnp.bfloat16), backward_total_sum.astype(jnp.bfloat16), jnp.stack(tap_grads))

def reference(clip_frames, spatial_weight, norm_gain, norm_bias, temporal_weight, cotangent):
    kernel = spatial_weight.reshape(-1, spatial_weight.shape[-1])

    def one_clip(pair):
        frames_in, upstream = pair
        patches = gather_patches(frames_in)
        flat = patches.reshape(-1, patches.shape[-1])
        out_shape = patches.shape[:-1] + (kernel.shape[1],)
        conv_out = jnp.dot(flat, kernel, preferred_element_type=jnp.float32).reshape(out_shape)
        activated, pullback = jax.vjp(activate, conv_out, norm_gain, norm_bias)
        acts = activated.astype(jnp.bfloat16)
        mixed, act_grad, temporal_part = temporal_pass(acts, upstream, temporal_weight)
        conv_grad, gain_partial_sum, bias_part = pullback(act_grad.astype(jnp.float32))
        conv_grad = conv_grad.astype(jnp.bfloat16).reshape(-1, kernel.shape[1])
        spatial_part = lax.dot_general(flat, conv_grad, (((0,), (0,)), ((), ())), preferred_element_type=jnp.float32)
        return (mixed, spatial_part, gain_partial_sum, bias_part, temporal_part)
    results = lax.map(one_clip, (clip_frames, cotangent))
    spatial_grad = lax.optimization_barrier(jnp.sum(results[1], axis=0)).reshape(spatial_weight.shape)
    return (results[0], spatial_grad, lax.optimization_barrier(jnp.sum(results[2], axis=0)), lax.optimization_barrier(jnp.sum(results[3], axis=0)), lax.optimization_barrier(jnp.sum(results[4], axis=0)))
```

```python
import functools

import jax
import jax.numpy as jnp
from jax import lax
from jax.experimental import pallas as pl
from jax.experimental.pallas import tpu as pltpu
from jax.sharding import PartitionSpec as P

GROUPS = 32
DILATION_FRAMES = 4
STREAMS = 4
CHUNKS = 8
LEAD = 8

MESH = pl.DeviceIdType.MESH
F32 = jnp.float32
BF16 = jnp.bfloat16

epsilon = 1e-05


def index_groups(clip_size, tm_size):
    clip_bits = [1 << k for k in range(clip_size.bit_length() - 1)]
    tm_bits = [1 << k for k in range(tm_size.bit_length() - 1)]
    groups = [("clip", clip_bits[:1])] if clip_bits else []
    groups += [("tm", tm_bits[k : k + 2]) for k in range(0, len(tm_bits), 2)]
    groups += [("clip", clip_bits[k : k + 2]) for k in range(1, len(clip_bits), 2)]
    return groups


def group_sum(values, width):
    lanes = values.shape[1]
    lane = lax.broadcasted_iota(jnp.int32, values.shape, 1)
    step = 1
    while step < width:
        before = pltpu.roll(values, step, 1)
        after = pltpu.roll(values, lanes - step, 1)
        values = values + jnp.where((lane // step) % 2 == 1, before, after)
        step *= 2
    return values


def fold(values):
    rows, chans = values.shape
    return jnp.sum(values.reshape(rows // 8, 8, chans), axis=0)


def spread(values):
    return jnp.broadcast_to(jnp.sum(values, axis=0, keepdims=True), values.shape)


def nt_dot(lhs, rhs):
    return lax.dot_general(lhs, rhs, (((1,), (1,)), ((), ())), preferred_element_type=F32)


def dot(lhs, rhs):
    return jnp.dot(lhs, rhs, preferred_element_type=F32)


def block_kernel(
    groups,
    tm_size,
    frames_hbm,
    kernel_hbm,
    gain_ref,
    bias_ref,
    mixer_hbm,
    cot_hbm,
    mixed_hbm,
    out_ref,
    raw,
    wide,
    even_rows,
    odd_rows,
    even_turned,
    odd_turned,
    normed,
    slope,
    acts,
    acts_turned,
    cot,
    near_cot,
    far_cot,
    near_acts,
    far_acts,
    soft_grad,
    conv_grad,
    mixed,
    kernel,
    mixer,
    acc,
    outgoing,
    incoming,
    local_sem,
    mixed_sem,
    shift_send,
    shift_recv,
    rs_send,
    rs_recv,
    ag_send,
    ag_recv,
):
    clip, place_tm = lax.axis_index("clip"), lax.axis_index("tm")
    place = {"clip": clip, "tm": place_tm}
    frames, height, width, in_chans = raw.shape
    rows, cols = height // 2, width // 2
    pixels = rows * cols
    chans = acts.shape[1]
    group = chans // GROUPS
    tile = frames * pixels // CHUNKS
    per_frame = CHUNKS // frames
    tile_rows = tile // cols
    taps = 3 * in_chans
    hop = DILATION_FRAMES // frames

    digits, peers = [], []
    for axis, weights in groups:
        bits = [(place[axis] // weight) % 2 for weight in weights]
        digits.append(sum(bit * (1 << k) for k, bit in enumerate(bits)))
        members = []
        for flip in range(1, 1 << len(weights)):
            other, digit = place[axis], 0
            for k, weight in enumerate(weights):
                flipped = (flip >> k) & 1
                other = other + flipped * weight * (1 - 2 * bits[k])
                digit = digit + (1 << k) * (1 - bits[k] if flipped else bits[k])
            device = (other, place_tm) if axis == "clip" else (clip, other)
            members.append((device, digit))
        peers.append(members)

    upper_bit = (place_tm // hop) % 2
    upper, lower = upper_bit == 1, upper_bit == 0
    has_far_cot = place_tm + 2 * hop < tm_size
    has_far_acts = place_tm >= 2 * hop
    has_near_cot = place_tm + hop < tm_size
    has_near_acts = place_tm >= hop
    ahead = (clip, (place_tm + 2 * hop) % tm_size)
    behind = (clip, (place_tm + tm_size - 2 * hop) % tm_size)
    partner = (clip, place_tm + hop * (1 - 2 * upper_bit))

    barrier = pltpu.get_barrier_semaphore()
    greeted = [device for members in peers for device, _ in members] + [ahead, behind]
    for device in greeted:
        pl.semaphore_signal(barrier, inc=1, device_id=device, device_id_type=MESH)

    loads = []
    for source, target in (
        [(kernel_hbm, kernel)]
        + [(frames_hbm.at[f], raw.at[f]) for f in range(frames)]
        + [(cot_hbm, cot), (mixer_hbm, mixer)]
    ):
        loads.append(pltpu.make_async_copy(source, target, local_sem.at[len(loads)]))
        loads[-1].start()
    load_kernel, load_frames, load_cot, load_mixer = loads[0], loads[1:-2], loads[-2], loads[-1]

    pl.semaphore_wait(barrier, len(greeted))

    def chunk(k):
        return pl.ds(pl.multiple_of(k * tile, tile), tile)

    def shift(kind, k, source, target, device):
        return pltpu.make_async_remote_copy(
            src_ref=source.at[chunk(k)],
            dst_ref=target.at[chunk(k)],
            send_sem=shift_send.at[kind, k],
            recv_sem=shift_recv.at[kind, k],
            device_id=device,
            device_id_type=MESH,
        )

    def far_cot_copy(k):
        return shift(0, k, cot_hbm, far_cot, behind)

    def near_cot_copy(k, source):
        return shift(1, k, source, near_cot, partner)

    def far_acts_copy(k):
        return shift(2, k, acts, far_acts, ahead)

    def near_acts_copy(k, source):
        return shift(3, k, source, near_acts, partner)

    @pl.when(has_far_acts)
    def _():
        for k in range(CHUNKS):
            far_cot_copy(k).start()

    @pl.when(upper)
    def _():
        for k in range(CHUNKS):
            near_cot_copy(k, cot_hbm).start()

    def clear(target):
        target[...] = jnp.zeros(target.shape, target.dtype)

    for present, target in (
        (has_far_cot, far_cot),
        (has_near_cot, near_cot),
        (has_far_acts, far_acts),
        (has_near_acts, near_acts),
    ):

        @pl.when(jnp.logical_not(present))
        def _(target=target):
            clear(target)

    def take_far_cot(k):
        @pl.when(has_far_cot)
        def _():
            far_cot_copy(k).wait_recv()

            @pl.when(lower)
            def _():
                near_cot_copy(k, far_cot).start()

    wide[:, 0:LEAD, :] = jnp.zeros((wide.shape[0], LEAD, in_chans), F32)
    for f in range(frames):
        odd_rows[f, 0] = jnp.zeros((cols, taps), BF16)
    conv_grad[pixels:] = jnp.zeros((cols, chans), BF16)
    gain = jnp.broadcast_to(gain_ref[...], (8, chans))
    bias = jnp.broadcast_to(bias_ref[...], (8, chans))
    count = pixels * group

    def rowwise(values):
        return jnp.broadcast_to(values[0:1], (tile, chans))

    scales = []
    step_rows = wide.shape[0]
    load_kernel.wait()
    for f in range(frames):
        load_frames[f].wait()

        def spread_columns(i, carry, f=f):
            first = pl.multiple_of(i * step_rows, step_rows)
            wide[:, LEAD : LEAD + width, :] = raw[f, pl.ds(first, step_rows)].astype(F32)
            parts = [wide[:, pl.ds(LEAD - 1 + j, cols, stride=2), :].astype(BF16) for j in range(3)]
            for r in range(step_rows):
                o = i * (step_rows // 2) + r // 2
                for j in range(3):
                    lanes = slice(j * in_chans, (j + 1) * in_chans)
                    if r % 2 == 0:
                        even_rows[f, o, :, lanes] = parts[j][r]
                    else:
                        odd_rows[f, o + 1, :, lanes] = parts[j][r]
            return carry

        lax.fori_loop(0, height // step_rows, spread_columns, 0)

        def convolve(q, total, f=f):
            first = q * tile_rows
            above = odd_rows[f, pl.ds(first, tile_rows)].reshape(tile, taps)
            here = even_rows[f, pl.ds(first, tile_rows)].reshape(tile, taps)
            below = odd_rows[f, pl.ds(first + 1, tile_rows)].reshape(tile, taps)
            conv = (
                dot(above, kernel[0:taps])
                + dot(here, kernel[taps : 2 * taps])
                + dot(below, kernel[2 * taps : 3 * taps])
            )
            normed[chunk(f * per_frame + q)] = conv
            return total + fold(conv)

        zero = jnp.zeros((8, chans), F32)
        total = lax.fori_loop(0, per_frame, convolve, zero)
        center = group_sum(spread(total), group) / count

        def square(q, total, f=f, center=center):
            deviation = normed[chunk(f * per_frame + q)] - rowwise(center)
            return total + fold(deviation * deviation)

        squares = lax.fori_loop(0, per_frame, square, zero)
        scale = lax.rsqrt(group_sum(spread(squares), group) / count + epsilon)
        scales.append(scale)

        def activate(q, carry, f=f, center=center, scale=scale):
            at = chunk(f * per_frame + q)
            value = (normed[at] - rowwise(center)) * rowwise(scale)
            normed[at] = value
            value = value * rowwise(gain) + rowwise(bias)
            sigmoid = jax.nn.sigmoid(value)
            acts[at] = (value * sigmoid).astype(BF16)
            slope[at] = sigmoid * (1.0 + value * (1.0 - sigmoid))
            return carry

        lax.fori_loop(0, per_frame, activate, 0)

        @pl.when(has_far_cot)
        def _(f=f):
            for q in range(per_frame):
                far_acts_copy(f * per_frame + q).start()

        take_far_cot(f)

    load_cot.wait()
    load_mixer.wait()
    for f in range(frames):

        def turn(q, carry, f=f):
            first = q * tile_rows
            at = pl.ds(pl.multiple_of(q * tile, tile), tile)
            even_turned[f, :, at] = even_rows[f, pl.ds(first, tile_rows)].reshape(tile, taps).T
            odd_turned[f, :, at] = odd_rows[f, pl.ds(first + 1, tile_rows)].reshape(tile, taps).T
            acts_turned[f, :, at] = acts[chunk(f * per_frame + q)].T
            return carry

        lax.fori_loop(0, per_frame, turn, 0)

    streams, devices, unit, _ = acc.shape
    flat = acc.reshape(streams * devices * unit, chans)
    spatial_at, temporal_at = 0, 3 * taps
    last_at = temporal_at + 3 * chans

    ahead_by = frames
    gain_part, bias_part = zero, zero
    half = CHUNKS // 2
    for f in range(frames):

        def back(q, sums, f=f):
            k = f * per_frame + q

            @pl.when(k + ahead_by < CHUNKS)
            def _():
                take_far_cot(jnp.minimum(k + ahead_by, CHUNKS - 1))

            @pl.when(has_near_cot)
            def _():
                near_cot_copy(k, cot_hbm).wait_recv()

            if f * per_frame >= half:
                for part in range(2):
                    j = 2 * (k - half) + part

                    @pl.when(has_far_acts)
                    def _():
                        far_acts_copy(j).wait_recv()

                        @pl.when(upper)
                        def _():
                            near_acts_copy(j, far_acts).start()

                    @pl.when(lower)
                    def _():
                        near_acts_copy(j, acts).start()

            at = chunk(k)
            here = cot[at]
            grad = (
                here.astype(F32)
                + nt_dot(here, mixer[0])
                + nt_dot(near_cot[at], mixer[1])
                + nt_dot(far_cot[at], mixer[2])
            )
            grad = grad.astype(BF16).astype(F32) * slope[at]
            soft_grad[pl.ds(pl.multiple_of(q * tile, tile), tile)] = grad
            return sums[0] + fold(grad), sums[1] + fold(grad * normed[at])

        plain, weighted = lax.fori_loop(0, per_frame, back, (zero, zero))
        plain, weighted = spread(plain), spread(weighted)
        bias_part, gain_part = bias_part + plain, gain_part + weighted
        mean_plain = group_sum(plain * gain, group) / count
        mean_weighted = group_sum(weighted * gain, group) / count

        def through_norm(q, carry, f=f, mean_plain=mean_plain, mean_weighted=mean_weighted):
            at = pl.ds(pl.multiple_of(q * tile, tile), tile)
            value = (
                soft_grad[at] * rowwise(gain)
                - rowwise(mean_plain)
                - normed[chunk(f * per_frame + q)] * rowwise(mean_weighted)
            ) * rowwise(scales[f])
            conv_grad[at] = value.astype(BF16)
            return carry

        lax.fori_loop(0, per_frame, through_norm, 0)

        def put(row, value, f=f):
            at = slice(row, row + value.shape[0])
            flat[at] = value if f == 0 else flat[at] + value

        here = conv_grad[0:pixels]
        put(spatial_at, dot(odd_turned[f], conv_grad[cols : cols + pixels]))
        put(spatial_at + taps, dot(even_turned[f], here))
        put(spatial_at + 2 * taps, dot(odd_turned[f], here))
        whole = slice(f * pixels, (f + 1) * pixels)
        for tap, source in enumerate((cot, near_cot, far_cot)):
            put(temporal_at + tap * chans, dot(acts_turned[f], source[whole]))

    flat[last_at : last_at + 8] = jnp.concatenate(
        [gain_part[0:1], bias_part[0:1], jnp.zeros((6, chans), F32)]
    )
    flat[last_at + 8 :] = jnp.zeros((flat.shape[0] - last_at - 8, chans), F32)

    writes = []

    def mix(k):
        @pl.when(has_near_acts)
        def _():
            near_acts_copy(k, acts).wait_recv()

        at = slice(k * tile, (k + 1) * tile)
        here = acts[at]
        total = (
            here.astype(F32)
            + dot(here, mixer[0])
            + dot(near_acts[at], mixer[1])
            + dot(far_acts[at], mixer[2])
        )
        mixed[at] = total.astype(BF16)
        writes.append(pltpu.make_async_copy(mixed.at[at], mixed_hbm.at[at], mixed_sem.at[k]))
        writes[-1].start()

    order_of_mixing = iter(range(CHUNKS))

    def mix_next(number):
        for _ in range(number):
            k = next(order_of_mixing, None)
            if k is not None:
                mix(k)

    count_groups = len(groups)
    orders = [list(range(count_groups)) for _ in range(streams)]
    if count_groups > 2:
        for order in orders[1::2]:
            order[1], order[2] = 2, 1
    pieces, slots = [], []
    for order in orders:
        size, slot = devices, 0
        pieces.append([])
        slots.append([])
        for which in order:
            size //= len(peers[which]) + 1
            pieces[-1].append(size)
            slots[-1].append(slot)
            slot += size * len(peers[which])
    base = [0] * streams
    kept = [[] for _ in range(streams)]
    flying = [[] for _ in range(streams)]
    copies = []

    def send(stream, turn, index, source, target, sems):
        which = orders[stream][turn]
        sem = sum(len(members) for members in peers[:which]) + index
        copy = pltpu.make_async_remote_copy(
            src_ref=source,
            dst_ref=target,
            send_sem=sems[0].at[stream, sem],
            recv_sem=sems[1].at[stream, sem],
            device_id=peers[which][index][0],
            device_id_type=MESH,
        )
        copy.start()
        copies.append(copy)
        flying[stream].append(copy)

    def send_pieces(stream, turn):
        size = pieces[stream][turn]
        flying[stream] = []
        for index, (_, digit) in enumerate(peers[orders[stream][turn]]):
            slot = pl.ds(slots[stream][turn] + index * size, size)
            give = pl.ds(base[stream] + digit * size, size)
            outgoing[stream, slot] = acc[stream, give].astype(BF16)
            send(
                stream,
                turn,
                index,
                outgoing.at[stream, slot],
                incoming.at[stream, slot],
                (rs_send, rs_recv),
            )

    def add_pieces(stream, turn):
        which = orders[stream][turn]
        size = pieces[stream][turn]
        base[stream] = base[stream] + digits[which] * size
        keep = pl.ds(base[stream], size)
        for copy in flying[stream]:
            copy.wait_recv()
        total = acc[stream, keep]
        for index in range(len(peers[which])):
            slot = pl.ds(slots[stream][turn] + index * size, size)
            total = total + incoming[stream, slot].astype(F32)
        acc[stream, keep] = total
        kept[stream].append(base[stream])

    def send_held(stream, turn):
        held = out_ref.at[stream, pl.ds(kept[stream][turn], pieces[stream][turn])]
        flying[stream] = []
        for index in range(len(peers[orders[stream][turn]])):
            send(stream, turn, index, held, held, (ag_send, ag_recv))

    for stream in range(streams):
        send_pieces(stream, 0)
    for turn in range(count_groups):
        for stream in range(streams):
            add_pieces(stream, turn)
            if turn + 1 < count_groups:
                send_pieces(stream, turn + 1)
            else:
                own = pl.ds(base[stream], 1)
                out_ref[stream, own] = acc[stream, own].astype(BF16)
                send_held(stream, turn)
        mix_next(1)
    for turn in reversed(range(count_groups)):
        for stream in range(streams):
            for copy in flying[stream]:
                copy.wait_recv()
            if turn > 0:
                send_held(stream, turn - 1)
        if turn > 0:
            mix_next(1)
    mix_next(CHUNKS)
    for copy in copies:
        copy.wait_send()
    for copy in writes:
        copy.wait()

    for k in range(CHUNKS):

        @pl.when(has_far_acts)
        def _(k=k):
            far_cot_copy(k).wait_send()

        @pl.when(has_far_cot)
        def _(k=k):
            far_acts_copy(k).wait_send()

        @pl.when(jnp.logical_or(upper, has_far_cot))
        def _(k=k):
            near_cot_copy(k, cot_hbm).wait_send()

        @pl.when(jnp.logical_or(lower, has_far_acts))
        def _(k=k):
            near_acts_copy(k, acts).wait_send()


def per_device(clip_size, tm_size, clip_frames, spatial_weight, norm_gain, norm_bias, temporal_weight, cotangent):
    _, frames, height, width, in_chans = clip_frames.shape
    chans = spatial_weight.shape[-1]
    rows, cols = height // 2, width // 2
    pixels = rows * cols
    taps = 3 * in_chans
    devices = clip_size * tm_size
    groups = index_groups(clip_size, tm_size)
    exchanges = sum((1 << len(weights)) - 1 for _, weights in groups)
    total_rows = 3 * taps + 3 * chans + 2
    streams = STREAMS
    while streams > 1 and streams * devices * 16 >= 2 * total_rows:
        streams //= 2
    unit = -(-total_rows // (streams * devices * 16)) * 16
    shape = (streams, devices, unit, chans)
    flat = (frames * pixels, chans)
    hbm = pl.BlockSpec(memory_space=pl.ANY)
    vmem = pl.BlockSpec(memory_space=pltpu.VMEM)
    dma = pltpu.SemaphoreType.DMA
    mixed, total = pl.pallas_call(
        functools.partial(block_kernel, groups, tm_size),
        out_shape=(
            jax.ShapeDtypeStruct(flat, BF16),
            jax.ShapeDtypeStruct(shape, BF16),
        ),
        in_specs=[hbm, hbm, vmem, vmem, hbm, hbm],
        out_specs=(hbm, vmem),
        scratch_shapes=[
            pltpu.VMEM((frames, height, width, in_chans), BF16),
            pltpu.VMEM((4, LEAD + width, in_chans), F32),
            pltpu.VMEM((frames, rows, cols, taps), BF16),
            pltpu.VMEM((frames, rows + 1, cols, taps), BF16),
            pltpu.VMEM((frames, taps, pixels), BF16),
            pltpu.VMEM((frames, taps, pixels), BF16),
            pltpu.VMEM(flat, F32),
            pltpu.VMEM(flat, F32),
            pltpu.VMEM(flat, BF16),
            pltpu.VMEM((frames, chans, pixels), BF16),
        ]
        + [pltpu.VMEM(flat, BF16)] * 5
        + [
            pltpu.VMEM((pixels, chans), F32),
            pltpu.VMEM((pixels + cols, chans), BF16),
            pltpu.VMEM(flat, BF16),
            pltpu.VMEM((3 * taps, chans), BF16),
            pltpu.VMEM((3, chans, chans), BF16),
            pltpu.VMEM(shape, F32),
            pltpu.VMEM(shape, BF16),
            pltpu.VMEM(shape, BF16),
            dma((frames + 3,)),
            dma((CHUNKS,)),
            dma((4, CHUNKS)),
            dma((4, CHUNKS)),
        ]
        + [dma((streams, exchanges))] * 4,
        compiler_params=pltpu.CompilerParams(
            collective_id=0, has_side_effects=True, vmem_limit_bytes=56 * 1024 * 1024
        ),
    )(
        clip_frames[0],
        spatial_weight.reshape(3 * taps, chans),
        norm_gain[None],
        norm_bias[None],
        temporal_weight,
        cotangent.reshape(flat),
    )
    totals = total.reshape(-1, chans).astype(F32)
    spatial_rows = 3 * taps
    temporal_end = spatial_rows + 3 * chans
    return (
        mixed.reshape(cotangent.shape),
        totals[:spatial_rows].reshape(spatial_weight.shape),
        totals[temporal_end],
        totals[temporal_end + 1],
        totals[spatial_rows:temporal_end].reshape(temporal_weight.shape),
    )


def solution(mesh):
    return jax.shard_map(
        functools.partial(per_device, mesh.shape["clip"], mesh.shape["tm"]),
        mesh=mesh,
        in_specs=(
            P("clip", "tm", None, None, None),
            P(),
            P(),
            P(),
            P(),
            P("clip", "tm", None, None, None),
        ),
        out_specs=(P("clip", "tm", None, None, None), P(), P(), P(), P()),
        check_vma=False,
    )
```

```python
import functools

import jax
import jax.numpy as jnp
from jax import lax
from jax.experimental import pallas as pl
from jax.experimental.pallas import tpu as pltpu
from jax.sharding import PartitionSpec as P

GROUPS = 32
DILATION_FRAMES = 4
STREAMS = 4
CHUNKS = 8
LEAD = 8

MESH = pl.DeviceIdType.MESH
F32 = jnp.float32
BF16 = jnp.bfloat16

epsilon = 1e-05


def index_groups(clip_size, tm_size):
    clip_bits = [1 << k for k in range(clip_size.bit_length() - 1)]
    tm_bits = [1 << k for k in range(tm_size.bit_length() - 1)]
    groups = [("clip", clip_bits[:1])] if clip_bits else []
    groups += [("tm", tm_bits[k : k + 2]) for k in range(0, len(tm_bits), 2)]
    groups += [("clip", clip_bits[k : k + 2]) for k in range(1, len(clip_bits), 2)]
    return groups


def group_sum(values, width):
    lanes = values.shape[1]
    lane = lax.broadcasted_iota(jnp.int32, values.shape, 1)
    step = 1
    while step < width:
        before = pltpu.roll(values, step, 1)
        after = pltpu.roll(values, lanes - step, 1)
        values = values + jnp.where((lane // step) % 2 == 1, before, after)
        step *= 2
    return values


def fold(values):
    rows, chans = values.shape
    return jnp.sum(values.reshape(rows // 8, 8, chans), axis=0)


def spread(values):
    return jnp.broadcast_to(jnp.sum(values, axis=0, keepdims=True), values.shape)


def nt_dot(lhs, rhs):
    return lax.dot_general(lhs, rhs, (((1,), (1,)), ((), ())), preferred_element_type=F32)


def dot(lhs, rhs):
    return jnp.dot(lhs, rhs, preferred_element_type=F32)


def block_kernel(
    groups,
    tm_size,
    frames_hbm,
    kernel_hbm,
    gain_hbm,
    bias_hbm,
    mixer_hbm,
    cot_hbm,
    mixed_ref,
    out_ref,
    raw,
    wide,
    even_rows,
    odd_rows,
    even_turned,
    odd_turned,
    normed,
    slope,
    acts,
    acts_turned,
    cot,
    near_cot,
    far_cot,
    near_acts,
    far_acts,
    soft_grad,
    conv_grad,
    kernel,
    mixer,
    gain_ref,
    bias_ref,
    acc,
    outgoing,
    incoming,
    local_sem,
    shift_send,
    shift_recv,
    rs_send,
    rs_recv,
    ag_send,
    ag_recv,
):
    clip, place_tm = lax.axis_index("clip"), lax.axis_index("tm")
    place = {"clip": clip, "tm": place_tm}
    frames, height, width, in_chans = raw.shape
    rows, cols = height // 2, width // 2
    pixels = rows * cols
    chans = acts.shape[1]
    group = chans // GROUPS
    tile = frames * pixels // CHUNKS
    per_frame = CHUNKS // frames
    tile_rows = tile // cols
    taps = 3 * in_chans
    hop = DILATION_FRAMES // frames

    digits, peers = [], []
    for axis, weights in groups:
        bits = [(place[axis] // weight) % 2 for weight in weights]
        digits.append(sum(bit * (1 << k) for k, bit in enumerate(bits)))
        members = []
        for flip in range(1, 1 << len(weights)):
            other, digit = place[axis], 0
            for k, weight in enumerate(weights):
                flipped = (flip >> k) & 1
                other = other + flipped * weight * (1 - 2 * bits[k])
                digit = digit + (1 << k) * (1 - bits[k] if flipped else bits[k])
            device = (other, place_tm) if axis == "clip" else (clip, other)
            members.append((device, digit))
        peers.append(members)

    upper_bit = (place_tm // hop) % 2
    upper, lower = upper_bit == 1, upper_bit == 0
    has_far_cot = place_tm + 2 * hop < tm_size
    has_far_acts = place_tm >= 2 * hop
    has_near_cot = place_tm + hop < tm_size
    has_near_acts = place_tm >= hop
    ahead = (clip, (place_tm + 2 * hop) % tm_size)
    behind = (clip, (place_tm + tm_size - 2 * hop) % tm_size)
    partner = (clip, place_tm + hop * (1 - 2 * upper_bit))

    barrier = pltpu.get_barrier_semaphore()
    greeted = [device for members in peers for device, _ in members] + [ahead, behind]
    for device in greeted:
        pl.semaphore_signal(barrier, inc=1, device_id=device, device_id_type=MESH)

    loads = []
    for source, target in (
        [(kernel_hbm, kernel)]
        + [(frames_hbm.at[f], raw.at[f]) for f in range(frames)]
        + [(gain_hbm, gain_ref), (bias_hbm, bias_ref), (cot_hbm, cot), (mixer_hbm, mixer)]
    ):
        loads.append(pltpu.make_async_copy(source, target, local_sem.at[len(loads)]))
        loads[-1].start()
    load_kernel, load_frames, load_rest = loads[0], loads[1 : frames + 1], loads[frames + 1 :]

    pl.semaphore_wait(barrier, len(greeted))

    def chunk(k):
        return pl.ds(pl.multiple_of(k * tile, tile), tile)

    def shift(kind, k, source, target, device):
        return pltpu.make_async_remote_copy(
            src_ref=source.at[chunk(k)],
            dst_ref=target.at[chunk(k)],
            send_sem=shift_send.at[kind, k],
            recv_sem=shift_recv.at[kind, k],
            device_id=device,
            device_id_type=MESH,
        )

    def far_cot_copy(k):
        return shift(0, k, cot_hbm, far_cot, behind)

    def near_cot_copy(k, source):
        return shift(1, k, source, near_cot, partner)

    def far_acts_copy(k):
        return shift(2, k, acts, far_acts, ahead)

    def near_acts_copy(k, source):
        return shift(3, k, source, near_acts, partner)

    @pl.when(has_far_acts)
    def _():
        for k in range(CHUNKS):
            far_cot_copy(k).start()

    @pl.when(upper)
    def _():
        for k in range(CHUNKS):
            near_cot_copy(k, cot_hbm).start()

    def clear(target):
        target[...] = jnp.zeros(target.shape, target.dtype)

    for present, target in (
        (has_far_cot, far_cot),
        (has_near_cot, near_cot),
        (has_far_acts, far_acts),
        (has_near_acts, near_acts),
    ):

        @pl.when(jnp.logical_not(present))
        def _(target=target):
            clear(target)

    def take_far_cot(k):
        @pl.when(has_far_cot)
        def _():
            far_cot_copy(k).wait_recv()

            @pl.when(lower)
            def _():
                near_cot_copy(k, far_cot).start()

    def ship_upper(k):
        @pl.when(has_far_acts)
        def _():
            far_acts_copy(k).wait_recv()

            @pl.when(upper)
            def _():
                near_acts_copy(k, far_acts).start()

    def ship_lower(k):
        @pl.when(lower)
        def _():
            near_acts_copy(k, acts).start()

    wide[:, 0:LEAD, :] = jnp.zeros((wide.shape[0], LEAD, in_chans), F32)
    for f in range(frames):
        odd_rows[f, 0] = jnp.zeros((cols, taps), BF16)
    conv_grad[pixels:] = jnp.zeros((cols, chans), BF16)
    for load in load_rest:
        load.wait()
    gain = jnp.broadcast_to(gain_ref[...], (8, chans))
    bias = jnp.broadcast_to(bias_ref[...], (8, chans))
    count = pixels * group

    def rowwise(values):
        return jnp.broadcast_to(values[0:1], (tile, chans))

    scales = []
    step_rows = wide.shape[0]
    load_kernel.wait()
    for f in range(frames):
        load_frames[f].wait()

        def spread_columns(i, carry, f=f):
            first = pl.multiple_of(i * step_rows, step_rows)
            wide[:, LEAD : LEAD + width, :] = raw[f, pl.ds(first, step_rows)].astype(F32)
            parts = [wide[:, pl.ds(LEAD - 1 + j, cols, stride=2), :].astype(BF16) for j in range(3)]
            for r in range(step_rows):
                o = i * (step_rows // 2) + r // 2
                for j in range(3):
                    lanes = slice(j * in_chans, (j + 1) * in_chans)
                    if r % 2 == 0:
                        even_rows[f, o, :, lanes] = parts[j][r]
                    else:
                        odd_rows[f, o + 1, :, lanes] = parts[j][r]
            return carry

        lax.fori_loop(0, height // step_rows, spread_columns, 0)

        def convolve(q, total, f=f):
            first = q * tile_rows
            above = odd_rows[f, pl.ds(first, tile_rows)].reshape(tile, taps)
            here = even_rows[f, pl.ds(first, tile_rows)].reshape(tile, taps)
            below = odd_rows[f, pl.ds(first + 1, tile_rows)].reshape(tile, taps)
            conv = (
                dot(above, kernel[0:taps])
                + dot(here, kernel[taps : 2 * taps])
                + dot(below, kernel[2 * taps : 3 * taps])
            )
            normed[chunk(f * per_frame + q)] = conv
            return total + fold(conv)

        zero = jnp.zeros((8, chans), F32)
        total = lax.fori_loop(0, per_frame, convolve, zero)
        center = group_sum(spread(total), group) / count

        def square(q, total, f=f, center=center):
            deviation = normed[chunk(f * per_frame + q)] - rowwise(center)
            return total + fold(deviation * deviation)

        squares = lax.fori_loop(0, per_frame, square, zero)
        scale = lax.rsqrt(group_sum(spread(squares), group) / count + epsilon)
        scales.append(scale)

        def activate(q, carry, f=f, center=center, scale=scale):
            at = chunk(f * per_frame + q)
            value = (normed[at] - rowwise(center)) * rowwise(scale)
            normed[at] = value
            value = value * rowwise(gain) + rowwise(bias)
            sigmoid = jax.nn.sigmoid(value)
            acts[at] = (value * sigmoid).astype(BF16)
            slope[at] = sigmoid * (1.0 + value * (1.0 - sigmoid))
            return carry

        lax.fori_loop(0, per_frame, activate, 0)

        @pl.when(has_far_cot)
        def _(f=f):
            for q in range(per_frame):
                far_acts_copy(f * per_frame + q).start()

        take_far_cot(f)

    for f in range(frames):

        def turn(q, carry, f=f):
            first = q * tile_rows
            at = pl.ds(pl.multiple_of(q * tile, tile), tile)
            even_turned[f, :, at] = even_rows[f, pl.ds(first, tile_rows)].reshape(tile, taps).T
            odd_turned[f, :, at] = odd_rows[f, pl.ds(first + 1, tile_rows)].reshape(tile, taps).T
            acts_turned[f, :, at] = acts[chunk(f * per_frame + q)].T
            return carry

        lax.fori_loop(0, per_frame, turn, 0)

    streams, devices, unit, _ = acc.shape
    flat = acc.reshape(streams * devices * unit, chans)
    spatial_at, temporal_at = 0, 3 * taps
    last_at = temporal_at + 3 * chans

    ahead_by = frames
    gain_part, bias_part = zero, zero
    half = CHUNKS // 2
    for f in range(frames):

        def back(q, sums, f=f):
            k = f * per_frame + q

            @pl.when(k + ahead_by < CHUNKS)
            def _():
                take_far_cot(jnp.minimum(k + ahead_by, CHUNKS - 1))

            @pl.when(has_near_cot)
            def _():
                near_cot_copy(k, cot_hbm).wait_recv()

            if f * per_frame >= half:
                ship_upper(k - half)

                @pl.when(k > half)
                def _():
                    ship_lower(jnp.maximum(k - half - 1, 0))

            at = chunk(k)
            here = cot[at]
            grad = (
                here.astype(F32)
                + nt_dot(here, mixer[0])
                + nt_dot(near_cot[at], mixer[1])
                + nt_dot(far_cot[at], mixer[2])
            )
            grad = grad.astype(BF16).astype(F32) * slope[at]
            soft_grad[pl.ds(pl.multiple_of(q * tile, tile), tile)] = grad
            return sums[0] + fold(grad), sums[1] + fold(grad * normed[at])

        plain, weighted = lax.fori_loop(0, per_frame, back, (zero, zero))
        plain, weighted = spread(plain), spread(weighted)
        bias_part, gain_part = bias_part + plain, gain_part + weighted
        mean_plain = group_sum(plain * gain, group) / count
        mean_weighted = group_sum(weighted * gain, group) / count

        def through_norm(q, carry, f=f, mean_plain=mean_plain, mean_weighted=mean_weighted):
            at = pl.ds(pl.multiple_of(q * tile, tile), tile)
            value = (
                soft_grad[at] * rowwise(gain)
                - rowwise(mean_plain)
                - normed[chunk(f * per_frame + q)] * rowwise(mean_weighted)
            ) * rowwise(scales[f])
            conv_grad[at] = value.astype(BF16)
            return carry

        lax.fori_loop(0, per_frame, through_norm, 0)

        def put(row, value, f=f):
            at = slice(row, row + value.shape[0])
            flat[at] = value if f == 0 else flat[at] + value

        here = conv_grad[0:pixels]
        put(spatial_at, dot(odd_turned[f], conv_grad[cols : cols + pixels]))
        put(spatial_at + taps, dot(even_turned[f], here))
        put(spatial_at + 2 * taps, dot(odd_turned[f], here))
        whole = slice(f * pixels, (f + 1) * pixels)
        for tap, source in enumerate((cot, near_cot, far_cot)):
            put(temporal_at + tap * chans, dot(acts_turned[f], source[whole]))

    flat[last_at : last_at + 8] = jnp.concatenate(
        [gain_part[0:1], bias_part[0:1], jnp.zeros((6, chans), F32)]
    )
    flat[last_at + 8 :] = jnp.zeros((flat.shape[0] - last_at - 8, chans), F32)

    def mix(k):
        @pl.when(has_near_acts)
        def _():
            near_acts_copy(k, acts).wait_recv()

        at = slice(k * tile, (k + 1) * tile)
        here = acts[at]
        total = (
            here.astype(F32)
            + dot(here, mixer[0])
            + dot(near_acts[at], mixer[1])
            + dot(far_acts[at], mixer[2])
        )
        mixed_ref[at] = total.astype(BF16)

    to_mix = list(range(CHUNKS))
    to_ship_upper = list(range(half, CHUNKS))
    to_ship_lower = list(range(half - 1, CHUNKS))

    def ship_next():
        if to_ship_upper:
            ship_upper(to_ship_upper.pop(0))
        if to_ship_lower:
            ship_lower(to_ship_lower.pop(0))

    def mix_next(number):
        for k in to_mix[:number]:
            mix(k)
        del to_mix[:number]

    count_groups = len(groups)
    orders = [list(range(count_groups)) for _ in range(streams)]
    if count_groups > 2:
        for order in orders[1::2]:
            order[1], order[2] = 2, 1
    pieces, slots = [], []
    for order in orders:
        size, slot = devices, 0
        pieces.append([])
        slots.append([])
        for which in order:
            size //= len(peers[which]) + 1
            pieces[-1].append(size)
            slots[-1].append(slot)
            slot += size * len(peers[which])
    base = [0] * streams
    kept = [[] for _ in range(streams)]
    flying = [[] for _ in range(streams)]
    copies = []

    def send(stream, turn, index, source, target, sems):
        which = orders[stream][turn]
        sem = sum(len(members) for members in peers[:which]) + index
        copy = pltpu.make_async_remote_copy(
            src_ref=source,
            dst_ref=target,
            send_sem=sems[0].at[stream, sem],
            recv_sem=sems[1].at[stream, sem],
            device_id=peers[which][index][0],
            device_id_type=MESH,
        )
        copy.start()
        copies.append(copy)
        flying[stream].append(copy)

    def send_pieces(stream, turn):
        size = pieces[stream][turn]
        flying[stream] = []
        for index, (_, digit) in enumerate(peers[orders[stream][turn]]):
            slot = pl.ds(slots[stream][turn] + index * size, size)
            give = pl.ds(base[stream] + digit * size, size)
            outgoing[stream, slot] = acc[stream, give].astype(BF16)
            send(
                stream,
                turn,
                index,
                outgoing.at[stream, slot],
                incoming.at[stream, slot],
                (rs_send, rs_recv),
            )

    def add_pieces(stream, turn):
        which = orders[stream][turn]
        size = pieces[stream][turn]
        base[stream] = base[stream] + digits[which] * size
        keep = pl.ds(base[stream], size)
        for copy in flying[stream]:
            copy.wait_recv()
        total = acc[stream, keep]
        for index in range(len(peers[which])):
            slot = pl.ds(slots[stream][turn] + index * size, size)
            total = total + incoming[stream, slot].astype(F32)
        acc[stream, keep] = total
        kept[stream].append(base[stream])

    def send_held(stream, turn):
        held = out_ref.at[stream, pl.ds(kept[stream][turn], pieces[stream][turn])]
        flying[stream] = []
        for index in range(len(peers[orders[stream][turn]])):
            send(stream, turn, index, held, held, (ag_send, ag_recv))

    for stream in range(streams):
        send_pieces(stream, 0)
    for turn in range(count_groups):
        for stream in range(streams):
            add_pieces(stream, turn)
            if turn + 1 < count_groups:
                send_pieces(stream, turn + 1)
            else:
                own = pl.ds(base[stream], 1)
                out_ref[stream, own] = acc[stream, own].astype(BF16)
                send_held(stream, turn)
        ship_next()
        mix_next(1)
    for turn in reversed(range(count_groups)):
        for stream in range(streams):
            for copy in flying[stream]:
                copy.wait_recv()
            if turn > 0:
                send_held(stream, turn - 1)
        ship_next()
        if turn > 0:
            mix_next(1)
    while to_ship_lower:
        ship_next()
    mix_next(CHUNKS)
    for copy in copies:
        copy.wait_send()
    for k in range(CHUNKS):

        @pl.when(has_far_acts)
        def _(k=k):
            far_cot_copy(k).wait_send()

        @pl.when(has_far_cot)
        def _(k=k):
            far_acts_copy(k).wait_send()

        @pl.when(jnp.logical_or(upper, has_far_cot))
        def _(k=k):
            near_cot_copy(k, cot_hbm).wait_send()

        @pl.when(jnp.logical_or(lower, has_far_acts))
        def _(k=k):
            near_acts_copy(k, acts).wait_send()


def finish_kernel(spatial_rows, total_ref, mixed_ref, mixed_hbm, spatial_hbm, temporal_hbm, gain_ref, bias_ref, wide, sems):
    streams, devices, unit, chans = total_ref.shape
    rows = streams * devices * unit
    flat = total_ref.reshape(rows, chans)
    copies = [pltpu.make_async_copy(mixed_ref, mixed_hbm, sems.at[0])]
    copies[0].start()
    temporal_rows = temporal_hbm.shape[0]
    pieces = [(spatial_hbm, 0, k * spatial_rows // 3, spatial_rows // 3) for k in range(3)]
    pieces += [(temporal_hbm, spatial_rows, k * temporal_rows // 3, temporal_rows // 3) for k in range(3)]
    for target, first, start, size in pieces:
        at = slice(first + start, first + start + size)
        wide[at] = flat[at].astype(F32)
        copies.append(
            pltpu.make_async_copy(wide.at[at], target.at[start : start + size], sems.at[len(copies)])
        )
        copies[-1].start()
    last = spatial_rows + temporal_rows
    ends = flat[last : last + 16].astype(F32)
    gain_ref[...] = ends[0:1]
    bias_ref[...] = ends[1:2]
    for copy in copies:
        copy.wait()


def in_hbm(x):
    return pltpu.with_memory_space_constraint(x, pltpu.HBM)


def per_device(clip_size, tm_size, clip_frames, spatial_weight, norm_gain, norm_bias, temporal_weight, cotangent):
    _, frames, height, width, in_chans = clip_frames.shape
    chans = spatial_weight.shape[-1]
    rows, cols = height // 2, width // 2
    pixels = rows * cols
    taps = 3 * in_chans
    devices = clip_size * tm_size
    groups = index_groups(clip_size, tm_size)
    exchanges = sum((1 << len(weights)) - 1 for _, weights in groups)
    total_rows = 3 * taps + 3 * chans + 2
    streams = STREAMS
    while streams > 1 and streams * devices * 16 >= 2 * total_rows:
        streams //= 2
    unit = -(-total_rows // (streams * devices * 16)) * 16
    shape = (streams, devices, unit, chans)
    flat = (frames * pixels, chans)
    hbm = pl.BlockSpec(memory_space=pltpu.HBM)
    vmem = pl.BlockSpec(memory_space=pltpu.VMEM)
    dma = pltpu.SemaphoreType.DMA
    mixed, total = pl.pallas_call(
        functools.partial(block_kernel, groups, tm_size),
        out_shape=(
            jax.ShapeDtypeStruct(flat, BF16),
            jax.ShapeDtypeStruct(shape, BF16),
        ),
        in_specs=[hbm] * 6,
        out_specs=(vmem, vmem),
        scratch_shapes=[
            pltpu.VMEM((frames, height, width, in_chans), BF16),
            pltpu.VMEM((4, LEAD + width, in_chans), F32),
            pltpu.VMEM((frames, rows, cols, taps), BF16),
            pltpu.VMEM((frames, rows + 1, cols, taps), BF16),
            pltpu.VMEM((frames, taps, pixels), BF16),
            pltpu.VMEM((frames, taps, pixels), BF16),
            pltpu.VMEM(flat, F32),
            pltpu.VMEM(flat, F32),
            pltpu.VMEM(flat, BF16),
            pltpu.VMEM((frames, chans, pixels), BF16),
        ]
        + [pltpu.VMEM(flat, BF16)] * 5
        + [
            pltpu.VMEM((pixels, chans), F32),
            pltpu.VMEM((pixels + cols, chans), BF16),
            pltpu.VMEM((3 * taps, chans), BF16),
            pltpu.VMEM((3, chans, chans), BF16),
            pltpu.VMEM((1, chans), F32),
            pltpu.VMEM((1, chans), F32),
            pltpu.VMEM(shape, F32),
            pltpu.VMEM(shape, BF16),
            pltpu.VMEM(shape, BF16),
            dma((frames + 5,)),
            dma((4, CHUNKS)),
            dma((4, CHUNKS)),
        ]
        + [dma((streams, exchanges))] * 4,
        compiler_params=pltpu.CompilerParams(
            collective_id=0, has_side_effects=True, vmem_limit_bytes=44 * 1024 * 1024
        ),
    )(
        in_hbm(clip_frames[0]),
        in_hbm(spatial_weight.reshape(3 * taps, chans)),
        in_hbm(norm_gain[None]),
        in_hbm(norm_bias[None]),
        in_hbm(temporal_weight),
        in_hbm(cotangent.reshape(flat)),
    )
    spatial_rows, temporal_rows = 3 * taps, 3 * chans
    mixed, spatial, temporal, gain, bias = pl.pallas_call(
        functools.partial(finish_kernel, spatial_rows),
        out_shape=(
            jax.ShapeDtypeStruct(flat, BF16),
            jax.ShapeDtypeStruct((spatial_rows, chans), F32),
            jax.ShapeDtypeStruct((temporal_rows, chans), F32),
            jax.ShapeDtypeStruct((1, chans), F32),
            jax.ShapeDtypeStruct((1, chans), F32),
        ),
        in_specs=[vmem, vmem],
        out_specs=(hbm, hbm, hbm, vmem, vmem),
        scratch_shapes=[pltpu.VMEM((spatial_rows + temporal_rows, chans), F32), dma((7,))],
        compiler_params=pltpu.CompilerParams(vmem_limit_bytes=12 * 1024 * 1024),
    )(total, mixed)
    return (
        mixed.reshape(cotangent.shape),
        spatial.reshape(spatial_weight.shape),
        gain[0],
        bias[0],
        temporal.reshape(temporal_weight.shape),
    )


def solution(mesh):
    return jax.shard_map(
        functools.partial(per_device, mesh.shape["clip"], mesh.shape["tm"]),
        mesh=mesh,
        in_specs=(
            P("clip", "tm", None, None, None),
            P(),
            P(),
            P(),
            P(),
            P("clip", "tm", None, None, None),
        ),
        out_specs=(P("clip", "tm", None, None, None), P(), P(), P(), P()),
        check_vma=False,
    )
```

```python
import functools

import jax
import jax.numpy as jnp
from jax import lax
from jax.experimental import pallas as pl
from jax.experimental.pallas import tpu as pltpu
from jax.sharding import PartitionSpec as P

GROUPS = 32
DILATION_FRAMES = 4
STREAMS = 4
CHUNKS = 8
PARTS = 1
EARLY = 1
UPPER_FROM = 4
LOWER_FROM = 5
LEAD = 8

MESH = pl.DeviceIdType.MESH
F32 = jnp.float32
BF16 = jnp.bfloat16

epsilon = 1e-05


PLANS = "BABA"


def stream_plans(clip_size, tm_size, streams):
    clip_bits = [1 << k for k in range(clip_size.bit_length() - 1)]
    tm_bits = [1 << k for k in range(tm_size.bit_length() - 1)]
    first = [("clip", tuple(clip_bits[:1]))] if clip_bits else []
    rest = [("tm", tuple(tm_bits[k : k + 2])) for k in range(4, len(tm_bits), 2)]
    rest += [("clip", tuple(clip_bits[k : k + 2])) for k in range(1, len(clip_bits), 2)]
    low, high = ("tm", tuple(tm_bits[:2])), ("tm", tuple(tm_bits[2:4]))
    kinds = {
        "A": [low, high],
        "B": [high, low],
        "C": [("tm", tuple(tm_bits[:1])), ("tm", tuple(tm_bits[1:4]))],
        "D": [("tm", tuple(tm_bits[:1])), high, ("tm", tuple(tm_bits[1:2]))],
    }
    return [first + kinds[PLANS[k]] + rest for k in range(streams)]


def group_sum(values, width):
    lanes = values.shape[1]
    lane = lax.broadcasted_iota(jnp.int32, values.shape, 1)
    step = 1
    while step < width:
        before = pltpu.roll(values, step, 1)
        after = pltpu.roll(values, lanes - step, 1)
        values = values + jnp.where((lane // step) % 2 == 1, before, after)
        step *= 2
    return values


def fold(values):
    rows, chans = values.shape
    return jnp.sum(values.reshape(rows // 8, 8, chans), axis=0)


def spread(values):
    return jnp.broadcast_to(jnp.sum(values, axis=0, keepdims=True), values.shape)


def nt_dot(lhs, rhs):
    return lax.dot_general(lhs, rhs, (((1,), (1,)), ((), ())), preferred_element_type=F32)


def dot(lhs, rhs):
    return jnp.dot(lhs, rhs, preferred_element_type=F32)


def block_kernel(
    plans,
    tm_size,
    frames_hbm,
    kernel_hbm,
    gain_hbm,
    bias_hbm,
    mixer_hbm,
    cot_hbm,
    mixed_ref,
    out_ref,
    raw,
    wide,
    even_rows,
    odd_rows,
    even_turned,
    odd_turned,
    normed,
    slope,
    acts,
    acts_turned,
    cot,
    near_cot,
    far_cot,
    near_acts,
    far_acts,
    soft_grad,
    conv_grad,
    kernel,
    mixer,
    gain_ref,
    bias_ref,
    acc,
    outgoing,
    incoming,
    local_sem,
    shift_send,
    shift_recv,
    rs_send,
    rs_recv,
    ag_send,
    ag_recv,
    greeting,
):
    clip, place_tm = lax.axis_index("clip"), lax.axis_index("tm")
    place = {"clip": clip, "tm": place_tm}
    frames, height, width, in_chans = raw.shape
    rows, cols = height // 2, width // 2
    pixels = rows * cols
    chans = acts.shape[1]
    group = chans // GROUPS
    tile = frames * pixels // CHUNKS
    per_frame = CHUNKS // frames
    tile_rows = tile // cols
    taps = 3 * in_chans
    hop = DILATION_FRAMES // frames

    digits, peers = {}, {}
    for axis, weights in dict.fromkeys(group for plan in plans for group in plan):
        bits = [(place[axis] // weight) % 2 for weight in weights]
        digits[axis, weights] = sum(bit * (1 << k) for k, bit in enumerate(bits))
        members = {}
        for flip in range(1, 1 << len(weights)):
            other, digit = place[axis], 0
            for k, weight in enumerate(weights):
                flipped = (flip >> k) & 1
                other = other + flipped * weight * (1 - 2 * bits[k])
                digit = digit + (1 << k) * (1 - bits[k] if flipped else bits[k])
            device = (other, place_tm) if axis == "clip" else (clip, other)
            distance = sum(weight for k, weight in enumerate(weights) if (flip >> k) & 1)
            members[axis, distance] = (device, digit)
        peers[axis, weights] = members

    upper_bit = (place_tm // hop) % 2
    upper, lower = upper_bit == 1, upper_bit == 0
    has_far_cot = place_tm + 2 * hop < tm_size
    has_far_acts = place_tm >= 2 * hop
    has_near_cot = place_tm + hop < tm_size
    has_near_acts = place_tm >= hop
    ahead = (clip, (place_tm + 2 * hop) % tm_size)
    behind = (clip, (place_tm + tm_size - 2 * hop) % tm_size)
    partner = (clip, place_tm + hop * (1 - 2 * upper_bit))

    barrier = pltpu.get_barrier_semaphore()
    met = {name: device for members in peers.values() for name, (device, _) in members.items()}
    near_by = [
        device
        for (axis, distance), device in met.items()
        if distance & (distance - 1) == 0 and (axis == "clip" or distance not in (2 * hop, 4 * hop))
    ]
    greeters = len(near_by) + has_far_cot.astype(jnp.int32) + has_far_acts.astype(jnp.int32)

    def greet(semaphore):
        for device in near_by:
            pl.semaphore_signal(semaphore, inc=1, device_id=device, device_id_type=MESH)

        @pl.when(has_far_cot)
        def _():
            pl.semaphore_signal(semaphore, inc=1, device_id=ahead, device_id_type=MESH)

        @pl.when(has_far_acts)
        def _():
            pl.semaphore_signal(semaphore, inc=1, device_id=behind, device_id_type=MESH)

    greet(barrier)

    loads = []
    for source, target in (
        [(kernel_hbm, kernel)]
        + [(frames_hbm.at[f], raw.at[f]) for f in range(frames)]
        + [(gain_hbm, gain_ref), (bias_hbm, bias_ref), (cot_hbm, cot), (mixer_hbm, mixer)]
    ):
        loads.append(pltpu.make_async_copy(source, target, local_sem.at[len(loads)]))
        loads[-1].start()
    load_kernel, load_frames, load_rest = loads[0], loads[1 : frames + 1], loads[frames + 1 :]

    def chunk(k):
        return pl.ds(pl.multiple_of(k * tile, tile), tile)

    def shift(kind, k, source, target, device, parts=1, part=0):
        size = tile // parts
        at = pl.ds(pl.multiple_of(k * tile + part * size, size), size)
        return pltpu.make_async_remote_copy(
            src_ref=source.at[at],
            dst_ref=target.at[at],
            send_sem=shift_send.at[kind, k * PARTS + part],
            recv_sem=shift_recv.at[kind, k * PARTS + part],
            device_id=device,
            device_id_type=MESH,
        )

    def far_cot_copy(k, part):
        return shift(0, k, cot_hbm, far_cot, behind, PARTS, part)

    def near_cot_copy(k, source, part):
        return shift(1, k, source, near_cot, partner, PARTS, part)

    def far_acts_copy(k):
        return shift(2, k, acts, far_acts, ahead)

    def near_acts_copy(k, source):
        return shift(3, k, source, near_acts, partner)

    def clear(target):
        target[...] = jnp.zeros(target.shape, target.dtype)

    for present, target in (
        (has_far_cot, far_cot),
        (has_near_cot, near_cot),
        (has_far_acts, far_acts),
        (has_near_acts, near_acts),
    ):

        @pl.when(jnp.logical_not(present))
        def _(target=target):
            clear(target)

    def take_far_cot(k):
        for part in range(PARTS):

            @pl.when(has_far_cot)
            def _(part=part):
                far_cot_copy(k, part).wait_recv()

                @pl.when(lower)
                def _():
                    near_cot_copy(k, far_cot, part).start()

    def ship_upper(k):
        @pl.when(has_far_acts)
        def _():
            far_acts_copy(k).wait_recv()

            @pl.when(upper)
            def _():
                near_acts_copy(k, far_acts).start()

    def ship_lower(k):
        @pl.when(lower)
        def _():
            near_acts_copy(k, acts).start()

    wide[:, 0:LEAD, :] = jnp.zeros((wide.shape[0], LEAD, in_chans), F32)
    for f in range(frames):
        odd_rows[f, 0] = jnp.zeros((cols, taps), BF16)
    conv_grad[pixels:] = jnp.zeros((cols, chans), BF16)
    for load in load_rest:
        load.wait()
    gain = jnp.broadcast_to(gain_ref[...], (8, chans))
    bias = jnp.broadcast_to(bias_ref[...], (8, chans))
    count = pixels * group

    def rowwise(values):
        return jnp.broadcast_to(values[0:1], (tile, chans))

    def send_cot():
        pl.semaphore_wait(barrier, greeters)

        @pl.when(has_far_acts)
        def _():
            for k in range(CHUNKS):
                for part in range(PARTS):
                    far_cot_copy(k, part).start()

        @pl.when(upper)
        def _():
            for k in range(CHUNKS):
                for part in range(PARTS):
                    near_cot_copy(k, cot_hbm, part).start()

    def send_far_acts(f):
        @pl.when(has_far_cot)
        def _():
            for q in range(per_frame):
                far_acts_copy(f * per_frame + q).start()

    scales = []
    step_rows = wide.shape[0]
    zero = jnp.zeros((8, chans), F32)

    def convolve_frame(f):
        def spread_columns(i, carry):
            first = pl.multiple_of(i * step_rows, step_rows)
            wide[:, LEAD : LEAD + width, :] = raw[f, pl.ds(first, step_rows)].astype(F32)
            parts = [wide[:, pl.ds(LEAD - 1 + j, cols, stride=2), :].astype(BF16) for j in range(3)]
            for r in range(step_rows):
                o = i * (step_rows // 2) + r // 2
                for j in range(3):
                    lanes = slice(j * in_chans, (j + 1) * in_chans)
                    if r % 2 == 0:
                        even_rows[f, o, :, lanes] = parts[j][r]
                    else:
                        odd_rows[f, o + 1, :, lanes] = parts[j][r]
            return carry

        lax.fori_loop(0, height // step_rows, spread_columns, 0)

        def convolve(q, total):
            first = q * tile_rows
            above = odd_rows[f, pl.ds(first, tile_rows)].reshape(tile, taps)
            here = even_rows[f, pl.ds(first, tile_rows)].reshape(tile, taps)
            below = odd_rows[f, pl.ds(first + 1, tile_rows)].reshape(tile, taps)
            conv = (
                dot(above, kernel[0:taps])
                + dot(here, kernel[taps : 2 * taps])
                + dot(below, kernel[2 * taps : 3 * taps])
            )
            normed[chunk(f * per_frame + q)] = conv
            return total + fold(conv)

        if f == 0:
            load_kernel.wait()
        return lax.fori_loop(0, per_frame, convolve, zero)

    def activate_frame(f, total):
        center = group_sum(spread(total), group) / count

        def square(q, total):
            deviation = normed[chunk(f * per_frame + q)] - rowwise(center)
            return total + fold(deviation * deviation)

        squares = lax.fori_loop(0, per_frame, square, zero)
        scale = lax.rsqrt(group_sum(spread(squares), group) / count + epsilon)
        scales.append(scale)

        def activate(q, carry):
            at = chunk(f * per_frame + q)
            value = (normed[at] - rowwise(center)) * rowwise(scale)
            normed[at] = value
            value = value * rowwise(gain) + rowwise(bias)
            sigmoid = jax.nn.sigmoid(value)
            acts[at] = (value * sigmoid).astype(BF16)
            slope[at] = sigmoid * (1.0 + value * (1.0 - sigmoid))
            return carry

        lax.fori_loop(0, per_frame, activate, 0)

    send_cot()
    greet(greeting.at[0])
    for f in range(frames):
        load_frames[f].wait()
        if f == 1:
            take_far_cot(0)
        total = convolve_frame(f)
        activate_frame(f, total)
        if f == 0:
            for k in range(EARLY):
                ship_lower(k)
        send_far_acts(f)
        if f == 0:
            pl.semaphore_wait(greeting.at[0], greeters)
            greet(greeting.at[1])
    if frames == 1:
        take_far_cot(0)

    streams, devices, unit, _ = acc.shape
    flat = acc.reshape(streams * devices * unit, chans)
    spatial_at, temporal_at = 0, 3 * taps
    last_at = temporal_at + 3 * chans

    for f in range(frames):

        def turn(q, carry, f=f):
            first = q * tile_rows
            at = pl.ds(pl.multiple_of(q * tile, tile), tile)
            even_turned[f, :, at] = even_rows[f, pl.ds(first, tile_rows)].reshape(tile, taps).T
            odd_turned[f, :, at] = odd_rows[f, pl.ds(first + 1, tile_rows)].reshape(tile, taps).T
            acts_turned[f, :, at] = acts[chunk(f * per_frame + q)].T
            return carry

        lax.fori_loop(0, per_frame, turn, 0)
        if f == 0:
            take_far_cot(1)
    flat[temporal_at : temporal_at + chans] = sum(
        dot(acts_turned[f], cot[f * pixels : (f + 1) * pixels]) for f in range(frames)
    )
    flat[temporal_at + chans : last_at] = jnp.zeros((2 * chans, chans), F32)

    ahead_by = 2
    gain_part, bias_part = zero, zero
    for f in range(frames):

        def back(q, sums, f=f):
            k = f * per_frame + q

            @pl.when(k + ahead_by < CHUNKS)
            def _():
                take_far_cot(jnp.minimum(k + ahead_by, CHUNKS - 1))

            @pl.when(has_near_cot)
            def _():
                for part in range(PARTS):
                    near_cot_copy(k, cot_hbm, part).wait_recv()

            @pl.when(k >= UPPER_FROM)
            def _():
                ship_upper(jnp.maximum(k - UPPER_FROM, 0))

            @pl.when(k >= LOWER_FROM)
            def _():
                ship_lower(jnp.maximum(k - LOWER_FROM, 0) + EARLY)

            at = chunk(k)
            here = cot[at]
            grad = (
                here.astype(F32)
                + nt_dot(here, mixer[0])
                + nt_dot(near_cot[at], mixer[1])
                + nt_dot(far_cot[at], mixer[2])
            )
            turned = acts_turned[f, :, pl.ds(pl.multiple_of(q * tile, tile), tile)]
            for tap, source in ((1, near_cot), (2, far_cot)):
                into = slice(temporal_at + tap * chans, temporal_at + (tap + 1) * chans)
                flat[into] = flat[into] + dot(turned, source[at])
            grad = grad.astype(BF16).astype(F32) * slope[at]
            soft_grad[pl.ds(pl.multiple_of(q * tile, tile), tile)] = grad
            return sums[0] + fold(grad), sums[1] + fold(grad * normed[at])

        plain, weighted = lax.fori_loop(0, per_frame, back, (zero, zero))
        plain, weighted = spread(plain), spread(weighted)
        bias_part, gain_part = bias_part + plain, gain_part + weighted
        mean_plain = group_sum(plain * gain, group) / count
        mean_weighted = group_sum(weighted * gain, group) / count

        def through_norm(q, carry, f=f, mean_plain=mean_plain, mean_weighted=mean_weighted):
            at = pl.ds(pl.multiple_of(q * tile, tile), tile)
            value = (
                soft_grad[at] * rowwise(gain)
                - rowwise(mean_plain)
                - normed[chunk(f * per_frame + q)] * rowwise(mean_weighted)
            ) * rowwise(scales[f])
            conv_grad[at] = value.astype(BF16)
            return carry

        lax.fori_loop(0, per_frame, through_norm, 0)

        def put(row, value, f=f):
            at = slice(row, row + value.shape[0])
            flat[at] = value if f == 0 else flat[at] + value

        here = conv_grad[0:pixels]
        put(spatial_at, dot(odd_turned[f], conv_grad[cols : cols + pixels]))
        put(spatial_at + taps, dot(even_turned[f], here))
        put(spatial_at + 2 * taps, dot(odd_turned[f], here))

    flat[last_at : last_at + 8] = jnp.concatenate(
        [gain_part[0:1], bias_part[0:1], jnp.zeros((6, chans), F32)]
    )
    flat[last_at + 8 :] = jnp.zeros((flat.shape[0] - last_at - 8, chans), F32)

    def mix(k):
        @pl.when(has_near_acts)
        def _():
            near_acts_copy(k, acts).wait_recv()

        at = slice(k * tile, (k + 1) * tile)
        here = acts[at]
        total = (
            here.astype(F32)
            + dot(here, mixer[0])
            + dot(near_acts[at], mixer[1])
            + dot(far_acts[at], mixer[2])
        )
        mixed_ref[at] = total.astype(BF16)

    to_mix = list(range(CHUNKS))
    to_ship_upper = list(range(CHUNKS - UPPER_FROM, CHUNKS))
    to_ship_lower = list(range(CHUNKS - LOWER_FROM + EARLY, CHUNKS))

    def ship_next():
        if to_ship_upper:
            ship_upper(to_ship_upper.pop(0))
        if to_ship_lower:
            ship_lower(to_ship_lower.pop(0))

    def mix_next(number):
        for k in to_mix[:number]:
            mix(k)
        del to_mix[:number]

    turns = len(plans[0])
    pieces, slots, sem_at = [], [], []
    for plan in plans:
        size, slot, sem = devices, 0, 0
        pieces.append([])
        slots.append([])
        sem_at.append([])
        for which in plan:
            size //= len(peers[which]) + 1
            pieces[-1].append(size)
            slots[-1].append(slot)
            sem_at[-1].append(sem)
            slot += size * len(peers[which])
            sem += len(peers[which])
    base = [0] * streams
    kept = [[] for _ in range(streams)]
    flying = [[] for _ in range(streams)]
    copies = []

    def send(stream, turn, index, source, target, sems):
        sem = sem_at[stream][turn] + index
        copy = pltpu.make_async_remote_copy(
            src_ref=source,
            dst_ref=target,
            send_sem=sems[0].at[stream, sem],
            recv_sem=sems[1].at[stream, sem],
            device_id=list(peers[plans[stream][turn]].values())[index][0],
            device_id_type=MESH,
        )
        copy.start()
        copies.append(copy)
        flying[stream].append(copy)

    def send_pieces(stream, turn):
        size = pieces[stream][turn]
        flying[stream] = []
        for index, (_, digit) in enumerate(peers[plans[stream][turn]].values()):
            slot = pl.ds(slots[stream][turn] + index * size, size)
            give = pl.ds(base[stream] + digit * size, size)
            outgoing[stream, slot] = acc[stream, give].astype(BF16)
            send(
                stream,
                turn,
                index,
                outgoing.at[stream, slot],
                incoming.at[stream, slot],
                (rs_send, rs_recv),
            )

    def add_pieces(stream, turn):
        which = plans[stream][turn]
        size = pieces[stream][turn]
        base[stream] = base[stream] + digits[which] * size
        keep = pl.ds(base[stream], size)
        for copy in flying[stream]:
            copy.wait_recv()
        total = acc[stream, keep]
        for index in range(len(peers[which])):
            slot = pl.ds(slots[stream][turn] + index * size, size)
            total = total + incoming[stream, slot].astype(F32)
        acc[stream, keep] = total
        kept[stream].append(base[stream])

    def send_held(stream, turn):
        held = out_ref.at[stream, pl.ds(kept[stream][turn], pieces[stream][turn])]
        flying[stream] = []
        for index in range(len(peers[plans[stream][turn]])):
            send(stream, turn, index, held, held, (ag_send, ag_recv))

    pl.semaphore_wait(greeting.at[1], greeters)
    for stream in range(streams):
        send_pieces(stream, 0)
    for turn in range(turns):
        for stream in range(streams):
            add_pieces(stream, turn)
            if turn + 1 < turns:
                send_pieces(stream, turn + 1)
            else:
                own = pl.ds(base[stream], 1)
                out_ref[stream, own] = acc[stream, own].astype(BF16)
                send_held(stream, turn)
        ship_next()
        mix_next(1)
    for turn in reversed(range(turns)):
        for stream in range(streams):
            for copy in flying[stream]:
                copy.wait_recv()
            if turn > 0:
                send_held(stream, turn - 1)
        ship_next()
        if turn > 0:
            mix_next(1)
    while to_ship_lower:
        ship_next()
    mix_next(CHUNKS)
    for copy in copies:
        copy.wait_send()
    for k in range(CHUNKS):

        @pl.when(has_far_acts)
        def _(k=k):
            for part in range(PARTS):
                far_cot_copy(k, part).wait_send()

        @pl.when(jnp.logical_or(upper, has_far_cot))
        def _(k=k):
            for part in range(PARTS):
                near_cot_copy(k, cot_hbm, part).wait_send()

        @pl.when(has_far_cot)
        def _(k=k):
            far_acts_copy(k).wait_send()

        @pl.when(jnp.logical_or(lower, has_far_acts))
        def _(k=k):
            near_acts_copy(k, acts).wait_send()


def finish_kernel(spatial_rows, total_ref, mixed_ref, mixed_hbm, spatial_hbm, temporal_hbm, gain_ref, bias_ref, wide, sems):
    streams, devices, unit, chans = total_ref.shape
    rows = streams * devices * unit
    flat = total_ref.reshape(rows, chans)
    copies = [pltpu.make_async_copy(mixed_ref, mixed_hbm, sems.at[0])]
    copies[0].start()
    temporal_rows = temporal_hbm.shape[0]
    pieces = [(spatial_hbm, 0, k * spatial_rows // 3, spatial_rows // 3) for k in range(3)]
    pieces += [(temporal_hbm, spatial_rows, k * temporal_rows // 3, temporal_rows // 3) for k in range(3)]
    for target, first, start, size in pieces:
        at = slice(first + start, first + start + size)
        wide[at] = flat[at].astype(F32)
        copies.append(
            pltpu.make_async_copy(wide.at[at], target.at[start : start + size], sems.at[len(copies)])
        )
        copies[-1].start()
    last = spatial_rows + temporal_rows
    ends = flat[last : last + 16].astype(F32)
    gain_ref[...] = ends[0:1]
    bias_ref[...] = ends[1:2]
    for copy in copies:
        copy.wait()


def in_hbm(x):
    return pltpu.with_memory_space_constraint(x, pltpu.HBM)


def per_device(clip_size, tm_size, clip_frames, spatial_weight, norm_gain, norm_bias, temporal_weight, cotangent):
    _, frames, height, width, in_chans = clip_frames.shape
    chans = spatial_weight.shape[-1]
    rows, cols = height // 2, width // 2
    pixels = rows * cols
    taps = 3 * in_chans
    devices = clip_size * tm_size
    total_rows = 3 * taps + 3 * chans + 2
    streams = STREAMS
    while streams > 1 and streams * devices * 16 >= 2 * total_rows:
        streams //= 2
    unit = -(-total_rows // (streams * devices * 16)) * 16
    shape = (streams, devices, unit, chans)
    plans = stream_plans(clip_size, tm_size, streams)
    exchanges = max(sum((1 << len(weights)) - 1 for _, weights in plan) for plan in plans)
    flat = (frames * pixels, chans)
    hbm = pl.BlockSpec(memory_space=pltpu.HBM)
    vmem = pl.BlockSpec(memory_space=pltpu.VMEM)
    dma = pltpu.SemaphoreType.DMA
    mixed, total = pl.pallas_call(
        functools.partial(block_kernel, plans, tm_size),
        out_shape=(
            jax.ShapeDtypeStruct(flat, BF16),
            jax.ShapeDtypeStruct(shape, BF16),
        ),
        in_specs=[hbm] * 6,
        out_specs=(vmem, vmem),
        scratch_shapes=[
            pltpu.VMEM((frames, height, width, in_chans), BF16),
            pltpu.VMEM((4, LEAD + width, in_chans), F32),
            pltpu.VMEM((frames, rows, cols, taps), BF16),
            pltpu.VMEM((frames, rows + 1, cols, taps), BF16),
            pltpu.VMEM((frames, taps, pixels), BF16),
            pltpu.VMEM((frames, taps, pixels), BF16),
            pltpu.VMEM(flat, F32),
            pltpu.VMEM(flat, F32),
            pltpu.VMEM(flat, BF16),
            pltpu.VMEM((frames, chans, pixels), BF16),
        ]
        + [pltpu.VMEM(flat, BF16)] * 5
        + [
            pltpu.VMEM((pixels, chans), F32),
            pltpu.VMEM((pixels + cols, chans), BF16),
            pltpu.VMEM((3 * taps, chans), BF16),
            pltpu.VMEM((3, chans, chans), BF16),
            pltpu.VMEM((1, chans), F32),
            pltpu.VMEM((1, chans), F32),
            pltpu.VMEM(shape, F32),
            pltpu.VMEM(shape, BF16),
            pltpu.VMEM(shape, BF16),
            dma((frames + 5,)),
            dma((4, CHUNKS * PARTS)),
            dma((4, CHUNKS * PARTS)),
        ]
        + [dma((streams, exchanges))] * 4
        + [pltpu.SemaphoreType.REGULAR((2,))],
        compiler_params=pltpu.CompilerParams(
            collective_id=0, has_side_effects=True, vmem_limit_bytes=44 * 1024 * 1024
        ),
    )(
        in_hbm(clip_frames[0]),
        in_hbm(spatial_weight.reshape(3 * taps, chans)),
        in_hbm(norm_gain[None]),
        in_hbm(norm_bias[None]),
        in_hbm(temporal_weight),
        in_hbm(cotangent.reshape(flat)),
    )
    spatial_rows, temporal_rows = 3 * taps, 3 * chans
    mixed, spatial, temporal, gain, bias = pl.pallas_call(
        functools.partial(finish_kernel, spatial_rows),
        out_shape=(
            jax.ShapeDtypeStruct(flat, BF16),
            jax.ShapeDtypeStruct((spatial_rows, chans), F32),
            jax.ShapeDtypeStruct((temporal_rows, chans), F32),
            jax.ShapeDtypeStruct((1, chans), F32),
            jax.ShapeDtypeStruct((1, chans), F32),
        ),
        in_specs=[vmem, vmem],
        out_specs=(hbm, hbm, hbm, vmem, vmem),
        scratch_shapes=[pltpu.VMEM((spatial_rows + temporal_rows, chans), F32), dma((7,))],
        compiler_params=pltpu.CompilerParams(vmem_limit_bytes=12 * 1024 * 1024),
    )(total, mixed)
    return (
        mixed.reshape(cotangent.shape),
        spatial.reshape(spatial_weight.shape),
        gain[0],
        bias[0],
        temporal.reshape(temporal_weight.shape),
    )


def solution(mesh):
    return jax.shard_map(
        functools.partial(per_device, mesh.shape["clip"], mesh.shape["tm"]),
        mesh=mesh,
        in_specs=(
            P("clip", "tm", None, None, None),
            P(),
            P(),
            P(),
            P(),
            P("clip", "tm", None, None, None),
        ),
        out_specs=(P("clip", "tm", None, None, None), P(), P(), P(), P()),
        check_vma=False,
    )
```

```python
import functools

import jax
import jax.numpy as jnp
from jax import lax
from jax.experimental import pallas as pl
from jax.experimental.pallas import tpu as pltpu
from jax.sharding import PartitionSpec as P

GROUPS = 32
DILATION_FRAMES = 4
STREAMS = 4
CHUNKS = 8
PARTS = 1
EARLY = 1
UPPER_FROM = 4
LOWER_FROM = 5
LEAD = 8

MESH = pl.DeviceIdType.MESH
F32 = jnp.float32
BF16 = jnp.bfloat16

epsilon = 1e-05


PLANS = "BABA"


def stream_plans(clip_size, tm_size, streams):
    clip_bits = [1 << k for k in range(clip_size.bit_length() - 1)]
    tm_bits = [1 << k for k in range(tm_size.bit_length() - 1)]
    first = [("clip", tuple(clip_bits[:1]))] if clip_bits else []
    rest = [("tm", tuple(tm_bits[k : k + 2])) for k in range(4, len(tm_bits), 2)]
    rest += [("clip", tuple(clip_bits[k : k + 2])) for k in range(1, len(clip_bits), 2)]
    low, high = ("tm", tuple(tm_bits[:2])), ("tm", tuple(tm_bits[2:4]))
    kinds = {
        "A": [low, high],
        "B": [high, low],
        "C": [("tm", tuple(tm_bits[:1])), ("tm", tuple(tm_bits[1:4]))],
        "D": [("tm", tuple(tm_bits[:1])), high, ("tm", tuple(tm_bits[1:2]))],
    }
    return [first + kinds[PLANS[k]] + rest for k in range(streams)]


def group_sum(values, width):
    lanes = values.shape[1]
    lane = lax.broadcasted_iota(jnp.int32, values.shape, 1)
    step = 1
    while step < width:
        before = pltpu.roll(values, step, 1)
        after = pltpu.roll(values, lanes - step, 1)
        values = values + jnp.where((lane // step) % 2 == 1, before, after)
        step *= 2
    return values


def fold(values):
    rows, chans = values.shape
    return jnp.sum(values.reshape(rows // 8, 8, chans), axis=0)


def spread(values):
    return jnp.broadcast_to(jnp.sum(values, axis=0, keepdims=True), values.shape)


def nt_dot(lhs, rhs):
    return lax.dot_general(lhs, rhs, (((1,), (1,)), ((), ())), preferred_element_type=F32)


def dot(lhs, rhs):
    return jnp.dot(lhs, rhs, preferred_element_type=F32)


def block_kernel(
    plans,
    tm_size,
    frames_hbm,
    kernel_hbm,
    gain_hbm,
    bias_hbm,
    mixer_hbm,
    cot_hbm,
    mixed_ref,
    out_ref,
    raw,
    wide,
    even_rows,
    odd_rows,
    even_turned,
    odd_turned,
    normed,
    slope,
    acts,
    acts_turned,
    cot,
    near_cot,
    far_cot,
    near_acts,
    far_acts,
    soft_grad,
    conv_grad,
    mixed_sum,
    kernel,
    mixer,
    gain_ref,
    bias_ref,
    acc,
    outgoing,
    incoming,
    local_sem,
    shift_send,
    shift_recv,
    rs_send,
    rs_recv,
    ag_send,
    ag_recv,
    greeting,
):
    clip, place_tm = lax.axis_index("clip"), lax.axis_index("tm")
    place = {"clip": clip, "tm": place_tm}
    frames, height, width, in_chans = raw.shape
    rows, cols = height // 2, width // 2
    pixels = rows * cols
    chans = acts.shape[1]
    group = chans // GROUPS
    tile = frames * pixels // CHUNKS
    per_frame = CHUNKS // frames
    tile_rows = tile // cols
    taps = 3 * in_chans
    hop = DILATION_FRAMES // frames

    digits, peers = {}, {}
    for axis, weights in dict.fromkeys(group for plan in plans for group in plan):
        bits = [(place[axis] // weight) % 2 for weight in weights]
        digits[axis, weights] = sum(bit * (1 << k) for k, bit in enumerate(bits))
        members = {}
        for flip in range(1, 1 << len(weights)):
            other, digit = place[axis], 0
            for k, weight in enumerate(weights):
                flipped = (flip >> k) & 1
                other = other + flipped * weight * (1 - 2 * bits[k])
                digit = digit + (1 << k) * (1 - bits[k] if flipped else bits[k])
            device = (other, place_tm) if axis == "clip" else (clip, other)
            distance = sum(weight for k, weight in enumerate(weights) if (flip >> k) & 1)
            members[axis, distance] = (device, digit)
        peers[axis, weights] = members

    upper_bit = (place_tm // hop) % 2
    upper, lower = upper_bit == 1, upper_bit == 0
    has_far_cot = place_tm + 2 * hop < tm_size
    has_far_acts = place_tm >= 2 * hop
    has_near_cot = place_tm + hop < tm_size
    has_near_acts = place_tm >= hop
    ahead = (clip, (place_tm + 2 * hop) % tm_size)
    behind = (clip, (place_tm + tm_size - 2 * hop) % tm_size)
    partner = (clip, place_tm + hop * (1 - 2 * upper_bit))

    barrier = pltpu.get_barrier_semaphore()
    met = {name: device for members in peers.values() for name, (device, _) in members.items()}
    near_by = [
        device
        for (axis, distance), device in met.items()
        if distance & (distance - 1) == 0 and (axis == "clip" or distance not in (2 * hop, 4 * hop))
    ]
    greeters = len(near_by) + has_far_cot.astype(jnp.int32) + has_far_acts.astype(jnp.int32)

    def greet(semaphore):
        for device in near_by:
            pl.semaphore_signal(semaphore, inc=1, device_id=device, device_id_type=MESH)

        @pl.when(has_far_cot)
        def _():
            pl.semaphore_signal(semaphore, inc=1, device_id=ahead, device_id_type=MESH)

        @pl.when(has_far_acts)
        def _():
            pl.semaphore_signal(semaphore, inc=1, device_id=behind, device_id_type=MESH)

    greet(barrier)

    loads = []
    for source, target in (
        [(kernel_hbm, kernel)]
        + [(frames_hbm.at[f], raw.at[f]) for f in range(frames)]
        + [(gain_hbm, gain_ref), (bias_hbm, bias_ref), (cot_hbm, cot), (mixer_hbm, mixer)]
    ):
        loads.append(pltpu.make_async_copy(source, target, local_sem.at[len(loads)]))
        loads[-1].start()
    load_kernel, load_frames, load_rest = loads[0], loads[1 : frames + 1], loads[frames + 1 :]

    def chunk(k):
        return pl.ds(pl.multiple_of(k * tile, tile), tile)

    def shift(kind, k, source, target, device, parts=1, part=0):
        size = tile // parts
        at = pl.ds(pl.multiple_of(k * tile + part * size, size), size)
        return pltpu.make_async_remote_copy(
            src_ref=source.at[at],
            dst_ref=target.at[at],
            send_sem=shift_send.at[kind, k * PARTS + part],
            recv_sem=shift_recv.at[kind, k * PARTS + part],
            device_id=device,
            device_id_type=MESH,
        )

    def far_cot_copy(k, part):
        return shift(0, k, cot_hbm, far_cot, behind, PARTS, part)

    def near_cot_copy(k, source, part):
        return shift(1, k, source, near_cot, partner, PARTS, part)

    def far_acts_copy(k):
        return shift(2, k, acts, far_acts, ahead)

    def near_acts_copy(k, source):
        return shift(3, k, source, near_acts, partner)

    def clear(target):
        target[...] = jnp.zeros(target.shape, target.dtype)

    for present, target in (
        (has_far_cot, far_cot),
        (has_near_cot, near_cot),
        (has_far_acts, far_acts),
        (has_near_acts, near_acts),
    ):

        @pl.when(jnp.logical_not(present))
        def _(target=target):
            clear(target)

    def take_far_cot(k):
        for part in range(PARTS):

            @pl.when(has_far_cot)
            def _(part=part):
                far_cot_copy(k, part).wait_recv()

                @pl.when(lower)
                def _():
                    near_cot_copy(k, far_cot, part).start()

    def ship_upper(k):
        @pl.when(has_far_acts)
        def _():
            far_acts_copy(k).wait_recv()

            @pl.when(upper)
            def _():
                near_acts_copy(k, far_acts).start()

    def ship_lower(k):
        @pl.when(lower)
        def _():
            near_acts_copy(k, acts).start()

    wide[:, 0:LEAD, :] = jnp.zeros((wide.shape[0], LEAD, in_chans), F32)
    for f in range(frames):
        odd_rows[f, 0] = jnp.zeros((cols, taps), BF16)
    conv_grad[pixels:] = jnp.zeros((cols, chans), BF16)
    for load in load_rest:
        load.wait()
    gain = jnp.broadcast_to(gain_ref[...], (8, chans))
    bias = jnp.broadcast_to(bias_ref[...], (8, chans))
    count = pixels * group

    def rowwise(values):
        return jnp.broadcast_to(values[0:1], (tile, chans))

    def send_cot():
        pl.semaphore_wait(barrier, greeters)

        @pl.when(has_far_acts)
        def _():
            for k in range(CHUNKS):
                for part in range(PARTS):
                    far_cot_copy(k, part).start()

        @pl.when(upper)
        def _():
            for k in range(CHUNKS):
                for part in range(PARTS):
                    near_cot_copy(k, cot_hbm, part).start()

    def send_far_acts(f):
        @pl.when(has_far_cot)
        def _():
            for q in range(per_frame):
                far_acts_copy(f * per_frame + q).start()

    scales = []
    step_rows = wide.shape[0]
    zero = jnp.zeros((8, chans), F32)

    def convolve_frame(f):
        def spread_columns(i, carry):
            first = pl.multiple_of(i * step_rows, step_rows)
            wide[:, LEAD : LEAD + width, :] = raw[f, pl.ds(first, step_rows)].astype(F32)
            parts = [wide[:, pl.ds(LEAD - 1 + j, cols, stride=2), :].astype(BF16) for j in range(3)]
            for r in range(step_rows):
                o = i * (step_rows // 2) + r // 2
                for j in range(3):
                    lanes = slice(j * in_chans, (j + 1) * in_chans)
                    if r % 2 == 0:
                        even_rows[f, o, :, lanes] = parts[j][r]
                    else:
                        odd_rows[f, o + 1, :, lanes] = parts[j][r]
            return carry

        lax.fori_loop(0, height // step_rows, spread_columns, 0)

        def convolve(q, total):
            first = q * tile_rows
            above = odd_rows[f, pl.ds(first, tile_rows)].reshape(tile, taps)
            here = even_rows[f, pl.ds(first, tile_rows)].reshape(tile, taps)
            below = odd_rows[f, pl.ds(first + 1, tile_rows)].reshape(tile, taps)
            conv = (
                dot(above, kernel[0:taps])
                + dot(here, kernel[taps : 2 * taps])
                + dot(below, kernel[2 * taps : 3 * taps])
            )
            normed[chunk(f * per_frame + q)] = conv
            return total + fold(conv)

        if f == 0:
            load_kernel.wait()
        return lax.fori_loop(0, per_frame, convolve, zero)

    def activate_frame(f, total):
        center = group_sum(spread(total), group) / count

        def square(q, total):
            deviation = normed[chunk(f * per_frame + q)] - rowwise(center)
            return total + fold(deviation * deviation)

        squares = lax.fori_loop(0, per_frame, square, zero)
        scale = lax.rsqrt(group_sum(spread(squares), group) / count + epsilon)
        scales.append(scale)

        def activate(q, carry):
            at = chunk(f * per_frame + q)
            value = (normed[at] - rowwise(center)) * rowwise(scale)
            normed[at] = value
            value = value * rowwise(gain) + rowwise(bias)
            sigmoid = jax.nn.sigmoid(value)
            acts[at] = (value * sigmoid).astype(BF16)
            slope[at] = sigmoid * (1.0 + value * (1.0 - sigmoid))
            return carry

        lax.fori_loop(0, per_frame, activate, 0)

    send_cot()
    greet(greeting.at[0])
    for f in range(frames):
        load_frames[f].wait()
        if f == 1:
            take_far_cot(0)
        total = convolve_frame(f)
        activate_frame(f, total)
        if f == 0:
            for k in range(EARLY):
                ship_lower(k)
        send_far_acts(f)
        if f == 0:
            pl.semaphore_wait(greeting.at[0], greeters)
            greet(greeting.at[1])
    if frames == 1:
        take_far_cot(0)

    streams, devices, unit, _ = acc.shape
    flat = acc.reshape(streams * devices * unit, chans)
    spatial_at, temporal_at = 0, 3 * taps
    last_at = temporal_at + 3 * chans

    for f in range(frames):

        def turn(q, carry, f=f):
            first = q * tile_rows
            at = pl.ds(pl.multiple_of(q * tile, tile), tile)
            even_turned[f, :, at] = even_rows[f, pl.ds(first, tile_rows)].reshape(tile, taps).T
            odd_turned[f, :, at] = odd_rows[f, pl.ds(first + 1, tile_rows)].reshape(tile, taps).T
            here = acts[chunk(f * per_frame + q)]
            acts_turned[f, :, at] = here.T
            mixed_sum[chunk(f * per_frame + q)] = here.astype(F32) + dot(here, mixer[0])
            return carry

        lax.fori_loop(0, per_frame, turn, 0)
        if f == 0:
            take_far_cot(1)
    flat[temporal_at : temporal_at + chans] = sum(
        dot(acts_turned[f], cot[f * pixels : (f + 1) * pixels]) for f in range(frames)
    )
    flat[temporal_at + chans : last_at] = jnp.zeros((2 * chans, chans), F32)

    ahead_by = 2
    gain_part, bias_part = zero, zero
    for f in range(frames):

        def back(q, sums, f=f):
            k = f * per_frame + q

            @pl.when(k + ahead_by < CHUNKS)
            def _():
                take_far_cot(jnp.minimum(k + ahead_by, CHUNKS - 1))

            @pl.when(has_near_cot)
            def _():
                for part in range(PARTS):
                    near_cot_copy(k, cot_hbm, part).wait_recv()

            @pl.when(k >= UPPER_FROM)
            def _():
                ship_upper(jnp.maximum(k - UPPER_FROM, 0))
                there = chunk(jnp.maximum(k - UPPER_FROM, 0))
                mixed_sum[there] = mixed_sum[there] + dot(far_acts[there], mixer[2])

            @pl.when(k >= LOWER_FROM)
            def _():
                ship_lower(jnp.maximum(k - LOWER_FROM, 0) + EARLY)

            at = chunk(k)
            here = cot[at]
            grad = (
                here.astype(F32)
                + nt_dot(here, mixer[0])
                + nt_dot(near_cot[at], mixer[1])
                + nt_dot(far_cot[at], mixer[2])
            )
            turned = acts_turned[f, :, pl.ds(pl.multiple_of(q * tile, tile), tile)]
            for tap, source in ((1, near_cot), (2, far_cot)):
                into = slice(temporal_at + tap * chans, temporal_at + (tap + 1) * chans)
                flat[into] = flat[into] + dot(turned, source[at])
            grad = grad.astype(BF16).astype(F32) * slope[at]
            soft_grad[pl.ds(pl.multiple_of(q * tile, tile), tile)] = grad
            return sums[0] + fold(grad), sums[1] + fold(grad * normed[at])

        plain, weighted = lax.fori_loop(0, per_frame, back, (zero, zero))
        plain, weighted = spread(plain), spread(weighted)
        bias_part, gain_part = bias_part + plain, gain_part + weighted
        mean_plain = group_sum(plain * gain, group) / count
        mean_weighted = group_sum(weighted * gain, group) / count

        def through_norm(q, carry, f=f, mean_plain=mean_plain, mean_weighted=mean_weighted):
            at = pl.ds(pl.multiple_of(q * tile, tile), tile)
            value = (
                soft_grad[at] * rowwise(gain)
                - rowwise(mean_plain)
                - normed[chunk(f * per_frame + q)] * rowwise(mean_weighted)
            ) * rowwise(scales[f])
            conv_grad[at] = value.astype(BF16)
            return carry

        lax.fori_loop(0, per_frame, through_norm, 0)

        def put(row, value, f=f):
            at = slice(row, row + value.shape[0])
            flat[at] = value if f == 0 else flat[at] + value

        here = conv_grad[0:pixels]
        put(spatial_at, dot(odd_turned[f], conv_grad[cols : cols + pixels]))
        put(spatial_at + taps, dot(even_turned[f], here))
        put(spatial_at + 2 * taps, dot(odd_turned[f], here))

    flat[last_at : last_at + 8] = jnp.concatenate(
        [gain_part[0:1], bias_part[0:1], jnp.zeros((6, chans), F32)]
    )
    flat[last_at + 8 :] = jnp.zeros((flat.shape[0] - last_at - 8, chans), F32)

    def mix(k):
        @pl.when(has_near_acts)
        def _():
            near_acts_copy(k, acts).wait_recv()

        at = slice(k * tile, (k + 1) * tile)
        total = mixed_sum[at] + dot(near_acts[at], mixer[1])
        if k >= CHUNKS - UPPER_FROM:
            total = total + dot(far_acts[at], mixer[2])
        mixed_ref[at] = total.astype(BF16)

    to_mix = list(range(CHUNKS))
    to_ship_upper = list(range(CHUNKS - UPPER_FROM, CHUNKS))
    to_ship_lower = list(range(CHUNKS - LOWER_FROM + EARLY, CHUNKS))

    def ship_next():
        if to_ship_upper:
            ship_upper(to_ship_upper.pop(0))
        if to_ship_lower:
            ship_lower(to_ship_lower.pop(0))

    def mix_next(number):
        for k in to_mix[:number]:
            mix(k)
        del to_mix[:number]

    turns = len(plans[0])
    pieces, slots, sem_at = [], [], []
    for plan in plans:
        size, slot, sem = devices, 0, 0
        pieces.append([])
        slots.append([])
        sem_at.append([])
        for which in plan:
            size //= len(peers[which]) + 1
            pieces[-1].append(size)
            slots[-1].append(slot)
            sem_at[-1].append(sem)
            slot += size * len(peers[which])
            sem += len(peers[which])
    base = [0] * streams
    kept = [[] for _ in range(streams)]
    flying = [[] for _ in range(streams)]
    copies = []

    def send(stream, turn, index, source, target, sems):
        sem = sem_at[stream][turn] + index
        copy = pltpu.make_async_remote_copy(
            src_ref=source,
            dst_ref=target,
            send_sem=sems[0].at[stream, sem],
            recv_sem=sems[1].at[stream, sem],
            device_id=list(peers[plans[stream][turn]].values())[index][0],
            device_id_type=MESH,
        )
        copy.start()
        copies.append(copy)
        flying[stream].append(copy)

    def send_pieces(stream, turn):
        size = pieces[stream][turn]
        flying[stream] = []
        for index, (_, digit) in enumerate(peers[plans[stream][turn]].values()):
            slot = pl.ds(slots[stream][turn] + index * size, size)
            give = pl.ds(base[stream] + digit * size, size)
            outgoing[stream, slot] = acc[stream, give].astype(BF16)
            send(
                stream,
                turn,
                index,
                outgoing.at[stream, slot],
                incoming.at[stream, slot],
                (rs_send, rs_recv),
            )

    def add_pieces(stream, turn):
        which = plans[stream][turn]
        size = pieces[stream][turn]
        base[stream] = base[stream] + digits[which] * size
        keep = pl.ds(base[stream], size)
        for copy in flying[stream]:
            copy.wait_recv()
        total = acc[stream, keep]
        for index in range(len(peers[which])):
            slot = pl.ds(slots[stream][turn] + index * size, size)
            total = total + incoming[stream, slot].astype(F32)
        acc[stream, keep] = total
        kept[stream].append(base[stream])

    def send_held(stream, turn):
        held = out_ref.at[stream, pl.ds(kept[stream][turn], pieces[stream][turn])]
        flying[stream] = []
        for index in range(len(peers[plans[stream][turn]])):
            send(stream, turn, index, held, held, (ag_send, ag_recv))

    pl.semaphore_wait(greeting.at[1], greeters)
    for stream in range(streams):
        send_pieces(stream, 0)
    for turn in range(turns):
        for stream in range(streams):
            add_pieces(stream, turn)
            if turn + 1 < turns:
                send_pieces(stream, turn + 1)
            else:
                own = pl.ds(base[stream], 1)
                out_ref[stream, own] = acc[stream, own].astype(BF16)
                send_held(stream, turn)
        ship_next()
        mix_next(2)
    for turn in reversed(range(turns)):
        for stream in range(streams):
            for copy in flying[stream]:
                copy.wait_recv()
            if turn > 0:
                send_held(stream, turn - 1)
        ship_next()
        if turn > 0:
            mix_next(1)
    while to_ship_lower:
        ship_next()
    mix_next(CHUNKS)
    for copy in copies:
        copy.wait_send()
    for k in range(CHUNKS):

        @pl.when(has_far_acts)
        def _(k=k):
            for part in range(PARTS):
                far_cot_copy(k, part).wait_send()

        @pl.when(jnp.logical_or(upper, has_far_cot))
        def _(k=k):
            for part in range(PARTS):
                near_cot_copy(k, cot_hbm, part).wait_send()

        @pl.when(has_far_cot)
        def _(k=k):
            far_acts_copy(k).wait_send()

        @pl.when(jnp.logical_or(lower, has_far_acts))
        def _(k=k):
            near_acts_copy(k, acts).wait_send()


def finish_kernel(spatial_rows, total_ref, mixed_ref, mixed_hbm, spatial_hbm, temporal_hbm, gain_ref, bias_ref, wide, sems):
    streams, devices, unit, chans = total_ref.shape
    rows = streams * devices * unit
    flat = total_ref.reshape(rows, chans)
    copies = [pltpu.make_async_copy(mixed_ref, mixed_hbm, sems.at[0])]
    copies[0].start()
    temporal_rows = temporal_hbm.shape[0]
    pieces = [(spatial_hbm, 0, k * spatial_rows // 3, spatial_rows // 3) for k in range(3)]
    pieces += [(temporal_hbm, spatial_rows, k * temporal_rows // 3, temporal_rows // 3) for k in range(3)]
    for target, first, start, size in pieces:
        at = slice(first + start, first + start + size)
        wide[at] = flat[at].astype(F32)
        copies.append(
            pltpu.make_async_copy(wide.at[at], target.at[start : start + size], sems.at[len(copies)])
        )
        copies[-1].start()
    last = spatial_rows + temporal_rows
    ends = flat[last : last + 16].astype(F32)
    gain_ref[...] = ends[0:1]
    bias_ref[...] = ends[1:2]
    for copy in copies:
        copy.wait()


def in_hbm(x):
    return pltpu.with_memory_space_constraint(x, pltpu.HBM)


def per_device(clip_size, tm_size, clip_frames, spatial_weight, norm_gain, norm_bias, temporal_weight, cotangent):
    _, frames, height, width, in_chans = clip_frames.shape
    chans = spatial_weight.shape[-1]
    rows, cols = height // 2, width // 2
    pixels = rows * cols
    taps = 3 * in_chans
    devices = clip_size * tm_size
    total_rows = 3 * taps + 3 * chans + 2
    streams = STREAMS
    while streams > 1 and streams * devices * 16 >= 2 * total_rows:
        streams //= 2
    unit = -(-total_rows // (streams * devices * 16)) * 16
    shape = (streams, devices, unit, chans)
    plans = stream_plans(clip_size, tm_size, streams)
    exchanges = max(sum((1 << len(weights)) - 1 for _, weights in plan) for plan in plans)
    flat = (frames * pixels, chans)
    hbm = pl.BlockSpec(memory_space=pltpu.HBM)
    vmem = pl.BlockSpec(memory_space=pltpu.VMEM)
    dma = pltpu.SemaphoreType.DMA
    mixed, total = pl.pallas_call(
        functools.partial(block_kernel, plans, tm_size),
        out_shape=(
            jax.ShapeDtypeStruct(flat, BF16),
            jax.ShapeDtypeStruct(shape, BF16),
        ),
        in_specs=[hbm] * 6,
        out_specs=(vmem, vmem),
        scratch_shapes=[
            pltpu.VMEM((frames, height, width, in_chans), BF16),
            pltpu.VMEM((4, LEAD + width, in_chans), F32),
            pltpu.VMEM((frames, rows, cols, taps), BF16),
            pltpu.VMEM((frames, rows + 1, cols, taps), BF16),
            pltpu.VMEM((frames, taps, pixels), BF16),
            pltpu.VMEM((frames, taps, pixels), BF16),
            pltpu.VMEM(flat, F32),
            pltpu.VMEM(flat, F32),
            pltpu.VMEM(flat, BF16),
            pltpu.VMEM((frames, chans, pixels), BF16),
        ]
        + [pltpu.VMEM(flat, BF16)] * 5
        + [
            pltpu.VMEM((pixels, chans), F32),
            pltpu.VMEM((pixels + cols, chans), BF16),
            pltpu.VMEM(flat, F32),
            pltpu.VMEM((3 * taps, chans), BF16),
            pltpu.VMEM((3, chans, chans), BF16),
            pltpu.VMEM((1, chans), F32),
            pltpu.VMEM((1, chans), F32),
            pltpu.VMEM(shape, F32),
            pltpu.VMEM(shape, BF16),
            pltpu.VMEM(shape, BF16),
            dma((frames + 5,)),
            dma((4, CHUNKS * PARTS)),
            dma((4, CHUNKS * PARTS)),
        ]
        + [dma((streams, exchanges))] * 4
        + [pltpu.SemaphoreType.REGULAR((2,))],
        compiler_params=pltpu.CompilerParams(
            collective_id=0, has_side_effects=True, vmem_limit_bytes=44 * 1024 * 1024
        ),
    )(
        in_hbm(clip_frames[0]),
        in_hbm(spatial_weight.reshape(3 * taps, chans)),
        in_hbm(norm_gain[None]),
        in_hbm(norm_bias[None]),
        in_hbm(temporal_weight),
        in_hbm(cotangent.reshape(flat)),
    )
    spatial_rows, temporal_rows = 3 * taps, 3 * chans
    mixed, spatial, temporal, gain, bias = pl.pallas_call(
        functools.partial(finish_kernel, spatial_rows),
        out_shape=(
            jax.ShapeDtypeStruct(flat, BF16),
            jax.ShapeDtypeStruct((spatial_rows, chans), F32),
            jax.ShapeDtypeStruct((temporal_rows, chans), F32),
            jax.ShapeDtypeStruct((1, chans), F32),
            jax.ShapeDtypeStruct((1, chans), F32),
        ),
        in_specs=[vmem, vmem],
        out_specs=(hbm, hbm, hbm, vmem, vmem),
        scratch_shapes=[pltpu.VMEM((spatial_rows + temporal_rows, chans), F32), dma((7,))],
        compiler_params=pltpu.CompilerParams(vmem_limit_bytes=12 * 1024 * 1024),
    )(total, mixed)
    return (
        mixed.reshape(cotangent.shape),
        spatial.reshape(spatial_weight.shape),
        gain[0],
        bias[0],
        temporal.reshape(temporal_weight.shape),
    )


def solution(mesh):
    return jax.shard_map(
        functools.partial(per_device, mesh.shape["clip"], mesh.shape["tm"]),
        mesh=mesh,
        in_specs=(
            P("clip", "tm", None, None, None),
            P(),
            P(),
            P(),
            P(),
            P("clip", "tm", None, None, None),
        ),
        out_specs=(P("clip", "tm", None, None, None), P(), P(), P(), P()),
        check_vma=False,
    )
```

```python
import functools

import jax
import jax.numpy as jnp
from jax import lax
from jax.experimental import pallas as pl
from jax.experimental.pallas import tpu as pltpu
from jax.sharding import PartitionSpec as P

GROUPS = 32
DILATION_FRAMES = 4
STREAMS = 4
CHUNKS = 8
PARTS = 1
EARLY = 1
UPPER_FROM = 4
LOWER_FROM = 5
LEAD = 8

MESH = pl.DeviceIdType.MESH
F32 = jnp.float32
BF16 = jnp.bfloat16

epsilon = 1e-05


PLANS = "BABA"


def stream_plans(clip_size, tm_size, streams):
    clip_bits = [1 << k for k in range(clip_size.bit_length() - 1)]
    tm_bits = [1 << k for k in range(tm_size.bit_length() - 1)]
    first = [("clip", tuple(clip_bits[:1]))] if clip_bits else []
    rest = [("tm", tuple(tm_bits[k : k + 2])) for k in range(4, len(tm_bits), 2)]
    rest += [("clip", tuple(clip_bits[k : k + 2])) for k in range(1, len(clip_bits), 2)]
    low, high = ("tm", tuple(tm_bits[:2])), ("tm", tuple(tm_bits[2:4]))
    kinds = {
        "A": [low, high],
        "B": [high, low],
        "C": [("tm", tuple(tm_bits[:1])), ("tm", tuple(tm_bits[1:4]))],
        "D": [("tm", tuple(tm_bits[:1])), high, ("tm", tuple(tm_bits[1:2]))],
    }
    return [first + kinds[PLANS[k]] + rest for k in range(streams)]


def group_sum(values, width):
    lanes = values.shape[1]
    lane = lax.broadcasted_iota(jnp.int32, values.shape, 1)
    step = 1
    while step < width:
        before = pltpu.roll(values, step, 1)
        after = pltpu.roll(values, lanes - step, 1)
        values = values + jnp.where((lane // step) % 2 == 1, before, after)
        step *= 2
    return values


def fold(values):
    rows, chans = values.shape
    return jnp.sum(values.reshape(rows // 8, 8, chans), axis=0)


def spread(values):
    return jnp.broadcast_to(jnp.sum(values, axis=0, keepdims=True), values.shape)


def nt_dot(lhs, rhs):
    return lax.dot_general(lhs, rhs, (((1,), (1,)), ((), ())), preferred_element_type=F32)


def dot(lhs, rhs):
    return jnp.dot(lhs, rhs, preferred_element_type=F32)


def block_kernel(
    plans,
    tm_size,
    frames_hbm,
    kernel_hbm,
    gain_hbm,
    bias_hbm,
    mixer_hbm,
    cot_hbm,
    mixed_ref,
    out_ref,
    raw,
    wide,
    even_rows,
    odd_rows,
    even_turned,
    odd_turned,
    normed,
    slope,
    acts,
    acts_turned,
    cot,
    near_cot,
    far_cot,
    near_acts,
    far_acts,
    soft_grad,
    conv_grad,
    mixed_sum,
    kernel,
    mixer,
    gain_ref,
    bias_ref,
    acc,
    outgoing,
    incoming,
    local_sem,
    shift_send,
    shift_recv,
    rs_send,
    rs_recv,
    ag_send,
    ag_recv,
    greeting,
):
    clip, place_tm = lax.axis_index("clip"), lax.axis_index("tm")
    place = {"clip": clip, "tm": place_tm}
    frames, height, width, in_chans = raw.shape
    rows, cols = height // 2, width // 2
    pixels = rows * cols
    chans = acts.shape[1]
    group = chans // GROUPS
    tile = frames * pixels // CHUNKS
    per_frame = CHUNKS // frames
    tile_rows = tile // cols
    taps = 3 * in_chans
    hop = DILATION_FRAMES // frames

    digits, peers = {}, {}
    for axis, weights in dict.fromkeys(group for plan in plans for group in plan):
        bits = [(place[axis] // weight) % 2 for weight in weights]
        digits[axis, weights] = sum(bit * (1 << k) for k, bit in enumerate(bits))
        members = {}
        for flip in range(1, 1 << len(weights)):
            other, digit = place[axis], 0
            for k, weight in enumerate(weights):
                flipped = (flip >> k) & 1
                other = other + flipped * weight * (1 - 2 * bits[k])
                digit = digit + (1 << k) * (1 - bits[k] if flipped else bits[k])
            device = (other, place_tm) if axis == "clip" else (clip, other)
            distance = sum(weight for k, weight in enumerate(weights) if (flip >> k) & 1)
            members[axis, distance] = (device, digit)
        peers[axis, weights] = members

    upper_bit = (place_tm // hop) % 2
    upper, lower = upper_bit == 1, upper_bit == 0
    has_far_cot = place_tm + 2 * hop < tm_size
    has_far_acts = place_tm >= 2 * hop
    has_near_cot = place_tm + hop < tm_size
    has_near_acts = place_tm >= hop
    ahead = (clip, (place_tm + 2 * hop) % tm_size)
    behind = (clip, (place_tm + tm_size - 2 * hop) % tm_size)
    partner = (clip, place_tm + hop * (1 - 2 * upper_bit))

    barrier = pltpu.get_barrier_semaphore()
    met = {name: device for members in peers.values() for name, (device, _) in members.items()}
    near_by = [
        device
        for (axis, distance), device in met.items()
        if distance & (distance - 1) == 0 and (axis == "clip" or distance not in (2 * hop, 4 * hop))
    ]
    greeters = len(near_by) + has_far_cot.astype(jnp.int32) + has_far_acts.astype(jnp.int32)

    def greet(semaphore):
        for device in near_by:
            pl.semaphore_signal(semaphore, inc=1, device_id=device, device_id_type=MESH)

        @pl.when(has_far_cot)
        def _():
            pl.semaphore_signal(semaphore, inc=1, device_id=ahead, device_id_type=MESH)

        @pl.when(has_far_acts)
        def _():
            pl.semaphore_signal(semaphore, inc=1, device_id=behind, device_id_type=MESH)

    greet(barrier)

    loads = []
    for source, target in (
        [(kernel_hbm, kernel)]
        + [(frames_hbm.at[f], raw.at[f]) for f in range(frames)]
        + [(gain_hbm, gain_ref), (bias_hbm, bias_ref), (cot_hbm, cot), (mixer_hbm, mixer)]
    ):
        loads.append(pltpu.make_async_copy(source, target, local_sem.at[len(loads)]))
        loads[-1].start()
    load_kernel, load_frames, load_rest = loads[0], loads[1 : frames + 1], loads[frames + 1 :]

    def chunk(k):
        return pl.ds(pl.multiple_of(k * tile, tile), tile)

    def shift(kind, k, source, target, device, parts=1, part=0):
        size = tile // parts
        at = pl.ds(pl.multiple_of(k * tile + part * size, size), size)
        return pltpu.make_async_remote_copy(
            src_ref=source.at[at],
            dst_ref=target.at[at],
            send_sem=shift_send.at[kind, k * PARTS + part],
            recv_sem=shift_recv.at[kind, k * PARTS + part],
            device_id=device,
            device_id_type=MESH,
        )

    def far_cot_copy(k, part):
        return shift(0, k, cot_hbm, far_cot, behind, PARTS, part)

    def near_cot_copy(k, source, part):
        return shift(1, k, source, near_cot, partner, PARTS, part)

    def far_acts_copy(k):
        return shift(2, k, acts, far_acts, ahead)

    def near_acts_copy(k, source):
        return shift(3, k, source, near_acts, partner)

    def clear(target):
        target[...] = jnp.zeros(target.shape, target.dtype)

    for present, target in (
        (has_far_cot, far_cot),
        (has_near_cot, near_cot),
        (has_far_acts, far_acts),
        (has_near_acts, near_acts),
    ):

        @pl.when(jnp.logical_not(present))
        def _(target=target):
            clear(target)

    def take_far_cot(k):
        for part in range(PARTS):

            @pl.when(has_far_cot)
            def _(part=part):
                far_cot_copy(k, part).wait_recv()

                @pl.when(lower)
                def _():
                    near_cot_copy(k, far_cot, part).start()

    def ship_upper(k):
        @pl.when(has_far_acts)
        def _():
            far_acts_copy(k).wait_recv()

            @pl.when(upper)
            def _():
                near_acts_copy(k, far_acts).start()

    def ship_lower(k):
        @pl.when(lower)
        def _():
            near_acts_copy(k, acts).start()

    wide[:, 0:LEAD, :] = jnp.zeros((wide.shape[0], LEAD, in_chans), F32)
    for f in range(frames):
        odd_rows[f, 0] = jnp.zeros((cols, taps), BF16)
    conv_grad[pixels:] = jnp.zeros((cols, chans), BF16)
    for load in load_rest:
        load.wait()
    gain = jnp.broadcast_to(gain_ref[...], (8, chans))
    bias = jnp.broadcast_to(bias_ref[...], (8, chans))
    count = pixels * group

    def rowwise(values):
        return jnp.broadcast_to(values[0:1], (tile, chans))

    def send_cot():
        pl.semaphore_wait(barrier, greeters)

        @pl.when(has_far_acts)
        def _():
            for k in range(CHUNKS):
                for part in range(PARTS):
                    far_cot_copy(k, part).start()

        @pl.when(upper)
        def _():
            for k in range(CHUNKS):
                for part in range(PARTS):
                    near_cot_copy(k, cot_hbm, part).start()

    def send_far_acts(f):
        @pl.when(has_far_cot)
        def _():
            for q in range(per_frame):
                far_acts_copy(f * per_frame + q).start()

    scales = []
    step_rows = wide.shape[0]
    zero = jnp.zeros((8, chans), F32)

    def convolve_frame(f):
        def spread_columns(i, carry):
            first = pl.multiple_of(i * step_rows, step_rows)
            wide[:, LEAD : LEAD + width, :] = raw[f, pl.ds(first, step_rows)].astype(F32)
            parts = [wide[:, pl.ds(LEAD - 1 + j, cols, stride=2), :].astype(BF16) for j in range(3)]
            for r in range(step_rows):
                o = i * (step_rows // 2) + r // 2
                for j in range(3):
                    lanes = slice(j * in_chans, (j + 1) * in_chans)
                    if r % 2 == 0:
                        even_rows[f, o, :, lanes] = parts[j][r]
                    else:
                        odd_rows[f, o + 1, :, lanes] = parts[j][r]
            return carry

        lax.fori_loop(0, height // step_rows, spread_columns, 0)

        def convolve(q, total):
            first = q * tile_rows
            above = odd_rows[f, pl.ds(first, tile_rows)].reshape(tile, taps)
            here = even_rows[f, pl.ds(first, tile_rows)].reshape(tile, taps)
            below = odd_rows[f, pl.ds(first + 1, tile_rows)].reshape(tile, taps)
            conv = (
                dot(above, kernel[0:taps])
                + dot(here, kernel[taps : 2 * taps])
                + dot(below, kernel[2 * taps : 3 * taps])
            )
            normed[chunk(f * per_frame + q)] = conv
            return total + fold(conv)

        if f == 0:
            load_kernel.wait()
        return lax.fori_loop(0, per_frame, convolve, zero)

    def activate_frame(f, total):
        center = group_sum(spread(total), group) / count

        def square(q, total):
            deviation = normed[chunk(f * per_frame + q)] - rowwise(center)
            return total + fold(deviation * deviation)

        squares = lax.fori_loop(0, per_frame, square, zero)
        scale = lax.rsqrt(group_sum(spread(squares), group) / count + epsilon)
        scales.append(scale)

        def activate(q, carry):
            at = chunk(f * per_frame + q)
            value = (normed[at] - rowwise(center)) * rowwise(scale)
            normed[at] = value
            value = value * rowwise(gain) + rowwise(bias)
            sigmoid = jax.nn.sigmoid(value)
            acts[at] = (value * sigmoid).astype(BF16)
            slope[at] = sigmoid * (1.0 + value * (1.0 - sigmoid))
            return carry

        lax.fori_loop(0, per_frame, activate, 0)

    send_cot()
    greet(greeting.at[0])
    for f in range(frames):
        load_frames[f].wait()
        if f == 1:
            take_far_cot(0)
        total = convolve_frame(f)
        activate_frame(f, total)
        if f == 0:
            for k in range(EARLY):
                ship_lower(k)
        send_far_acts(f)
        if f == 0:
            pl.semaphore_wait(greeting.at[0], greeters)
            greet(greeting.at[1])
    if frames == 1:
        take_far_cot(0)

    streams, devices, unit, _ = acc.shape
    flat = acc.reshape(streams * devices * unit, chans)
    spatial_at, temporal_at = 0, 3 * taps
    last_at = temporal_at + 3 * chans

    for f in range(frames):

        def turn(q, carry, f=f):
            first = q * tile_rows
            at = pl.ds(pl.multiple_of(q * tile, tile), tile)
            even_turned[f, :, at] = even_rows[f, pl.ds(first, tile_rows)].reshape(tile, taps).T
            odd_turned[f, :, at] = odd_rows[f, pl.ds(first + 1, tile_rows)].reshape(tile, taps).T
            here = acts[chunk(f * per_frame + q)]
            acts_turned[f, :, at] = here.T
            mixed_sum[chunk(f * per_frame + q)] = here.astype(F32) + dot(here, mixer[0])
            return carry

        if f == 0:
            take_far_cot(1)
        lax.fori_loop(0, per_frame, turn, 0)
    flat[temporal_at : temporal_at + chans] = sum(
        dot(acts_turned[f], cot[f * pixels : (f + 1) * pixels]) for f in range(frames)
    )
    flat[temporal_at + chans : last_at] = jnp.zeros((2 * chans, chans), F32)

    ahead_by = 2
    gain_part, bias_part = zero, zero
    for f in range(frames):

        def back(q, sums, f=f):
            k = f * per_frame + q

            @pl.when(k + ahead_by < CHUNKS)
            def _():
                take_far_cot(jnp.minimum(k + ahead_by, CHUNKS - 1))

            @pl.when(has_near_cot)
            def _():
                for part in range(PARTS):
                    near_cot_copy(k, cot_hbm, part).wait_recv()

            @pl.when(k >= UPPER_FROM)
            def _():
                ship_upper(jnp.maximum(k - UPPER_FROM, 0))
                there = chunk(jnp.maximum(k - UPPER_FROM, 0))
                mixed_sum[there] = mixed_sum[there] + dot(far_acts[there], mixer[2])

            @pl.when(k >= LOWER_FROM)
            def _():
                ship_lower(jnp.maximum(k - LOWER_FROM, 0) + EARLY)

            at = chunk(k)
            here = cot[at]
            grad = (
                here.astype(F32)
                + nt_dot(here, mixer[0])
                + nt_dot(near_cot[at], mixer[1])
                + nt_dot(far_cot[at], mixer[2])
            )
            turned = acts_turned[f, :, pl.ds(pl.multiple_of(q * tile, tile), tile)]
            for tap, source in ((1, near_cot), (2, far_cot)):
                into = slice(temporal_at + tap * chans, temporal_at + (tap + 1) * chans)
                flat[into] = flat[into] + dot(turned, source[at])
            grad = grad.astype(BF16).astype(F32) * slope[at]
            soft_grad[pl.ds(pl.multiple_of(q * tile, tile), tile)] = grad
            return sums[0] + fold(grad), sums[1] + fold(grad * normed[at])

        plain, weighted = lax.fori_loop(0, per_frame, back, (zero, zero))
        plain, weighted = spread(plain), spread(weighted)
        bias_part, gain_part = bias_part + plain, gain_part + weighted
        mean_plain = group_sum(plain * gain, group) / count
        mean_weighted = group_sum(weighted * gain, group) / count

        def through_norm(q, carry, f=f, mean_plain=mean_plain, mean_weighted=mean_weighted):
            at = pl.ds(pl.multiple_of(q * tile, tile), tile)
            value = (
                soft_grad[at] * rowwise(gain)
                - rowwise(mean_plain)
                - normed[chunk(f * per_frame + q)] * rowwise(mean_weighted)
            ) * rowwise(scales[f])
            conv_grad[at] = value.astype(BF16)
            return carry

        lax.fori_loop(0, per_frame, through_norm, 0)

        def put(row, value, f=f):
            at = slice(row, row + value.shape[0])
            flat[at] = value if f == 0 else flat[at] + value

        here = conv_grad[0:pixels]
        put(spatial_at, dot(odd_turned[f], conv_grad[cols : cols + pixels]))
        put(spatial_at + taps, dot(even_turned[f], here))
        put(spatial_at + 2 * taps, dot(odd_turned[f], here))

    flat[last_at : last_at + 8] = jnp.concatenate(
        [gain_part[0:1], bias_part[0:1], jnp.zeros((6, chans), F32)]
    )
    flat[last_at + 8 :] = jnp.zeros((flat.shape[0] - last_at - 8, chans), F32)

    def mix(k):
        @pl.when(has_near_acts)
        def _():
            near_acts_copy(k, acts).wait_recv()

        at = slice(k * tile, (k + 1) * tile)
        total = mixed_sum[at] + dot(near_acts[at], mixer[1])
        if k >= CHUNKS - UPPER_FROM:
            total = total + dot(far_acts[at], mixer[2])
        mixed_ref[at] = total.astype(BF16)

    to_mix = list(range(CHUNKS))
    to_ship_upper = list(range(CHUNKS - UPPER_FROM, CHUNKS))
    to_ship_lower = list(range(CHUNKS - LOWER_FROM + EARLY, CHUNKS))

    def ship_next():
        if to_ship_upper:
            ship_upper(to_ship_upper.pop(0))
        if to_ship_lower:
            ship_lower(to_ship_lower.pop(0))

    def mix_next(number):
        for k in to_mix[:number]:
            mix(k)
        del to_mix[:number]

    turns = len(plans[0])
    pieces, slots, sem_at = [], [], []
    for plan in plans:
        size, slot, sem = devices, 0, 0
        pieces.append([])
        slots.append([])
        sem_at.append([])
        for which in plan:
            size //= len(peers[which]) + 1
            pieces[-1].append(size)
            slots[-1].append(slot)
            sem_at[-1].append(sem)
            slot += size * len(peers[which])
            sem += len(peers[which])
    base = [0] * streams
    kept = [[] for _ in range(streams)]
    flying = [[] for _ in range(streams)]
    copies = []

    def send(stream, turn, index, source, target, sems):
        sem = sem_at[stream][turn] + index
        copy = pltpu.make_async_remote_copy(
            src_ref=source,
            dst_ref=target,
            send_sem=sems[0].at[stream, sem],
            recv_sem=sems[1].at[stream, sem],
            device_id=list(peers[plans[stream][turn]].values())[index][0],
            device_id_type=MESH,
        )
        copy.start()
        copies.append(copy)
        flying[stream].append(copy)

    def send_pieces(stream, turn):
        size = pieces[stream][turn]
        flying[stream] = []
        for index, (_, digit) in enumerate(peers[plans[stream][turn]].values()):
            slot = pl.ds(slots[stream][turn] + index * size, size)
            give = pl.ds(base[stream] + digit * size, size)
            outgoing[stream, slot] = acc[stream, give].astype(BF16)
            send(
                stream,
                turn,
                index,
                outgoing.at[stream, slot],
                incoming.at[stream, slot],
                (rs_send, rs_recv),
            )

    def add_pieces(stream, turn):
        which = plans[stream][turn]
        size = pieces[stream][turn]
        base[stream] = base[stream] + digits[which] * size
        keep = pl.ds(base[stream], size)
        for copy in flying[stream]:
            copy.wait_recv()
        total = acc[stream, keep]
        for index in range(len(peers[which])):
            slot = pl.ds(slots[stream][turn] + index * size, size)
            total = total + incoming[stream, slot].astype(F32)
        acc[stream, keep] = total
        kept[stream].append(base[stream])

    def send_held(stream, turn):
        held = out_ref.at[stream, pl.ds(kept[stream][turn], pieces[stream][turn])]
        flying[stream] = []
        for index in range(len(peers[plans[stream][turn]])):
            send(stream, turn, index, held, held, (ag_send, ag_recv))

    pl.semaphore_wait(greeting.at[1], greeters)
    for stream in range(streams):
        send_pieces(stream, 0)
    for turn in range(turns):
        for stream in range(streams):
            add_pieces(stream, turn)
            if turn + 1 < turns:
                send_pieces(stream, turn + 1)
            else:
                own = pl.ds(base[stream], 1)
                out_ref[stream, own] = acc[stream, own].astype(BF16)
                send_held(stream, turn)
        ship_next()
        mix_next(2)
    for turn in reversed(range(turns)):
        for stream in range(streams):
            for copy in flying[stream]:
                copy.wait_recv()
            if turn > 0:
                send_held(stream, turn - 1)
        ship_next()
        if turn > 0:
            mix_next(1)
    while to_ship_lower:
        ship_next()
    mix_next(CHUNKS)
    for copy in copies:
        copy.wait_send()
    for k in range(CHUNKS):

        @pl.when(has_far_acts)
        def _(k=k):
            for part in range(PARTS):
                far_cot_copy(k, part).wait_send()

        @pl.when(jnp.logical_or(upper, has_far_cot))
        def _(k=k):
            for part in range(PARTS):
                near_cot_copy(k, cot_hbm, part).wait_send()

        @pl.when(has_far_cot)
        def _(k=k):
            far_acts_copy(k).wait_send()

        @pl.when(jnp.logical_or(lower, has_far_acts))
        def _(k=k):
            near_acts_copy(k, acts).wait_send()


def finish_kernel(spatial_rows, total_ref, mixed_ref, mixed_hbm, spatial_hbm, temporal_hbm, gain_ref, bias_ref, wide, sems):
    streams, devices, unit, chans = total_ref.shape
    rows = streams * devices * unit
    flat = total_ref.reshape(rows, chans)
    copies = [pltpu.make_async_copy(mixed_ref, mixed_hbm, sems.at[0])]
    copies[0].start()
    temporal_rows = temporal_hbm.shape[0]
    pieces = [(spatial_hbm, 0, k * spatial_rows // 3, spatial_rows // 3) for k in range(3)]
    pieces += [(temporal_hbm, spatial_rows, k * temporal_rows // 3, temporal_rows // 3) for k in range(3)]
    for target, first, start, size in pieces:
        at = slice(first + start, first + start + size)
        wide[at] = flat[at].astype(F32)
        copies.append(
            pltpu.make_async_copy(wide.at[at], target.at[start : start + size], sems.at[len(copies)])
        )
        copies[-1].start()
    last = spatial_rows + temporal_rows
    ends = flat[last : last + 16].astype(F32)
    gain_ref[...] = ends[0:1]
    bias_ref[...] = ends[1:2]
    for copy in copies:
        copy.wait()


def in_hbm(x):
    return pltpu.with_memory_space_constraint(x, pltpu.HBM)


def per_device(clip_size, tm_size, clip_frames, spatial_weight, norm_gain, norm_bias, temporal_weight, cotangent):
    _, frames, height, width, in_chans = clip_frames.shape
    chans = spatial_weight.shape[-1]
    rows, cols = height // 2, width // 2
    pixels = rows * cols
    taps = 3 * in_chans
    devices = clip_size * tm_size
    total_rows = 3 * taps + 3 * chans + 2
    streams = STREAMS
    while streams > 1 and streams * devices * 16 >= 2 * total_rows:
        streams //= 2
    unit = -(-total_rows // (streams * devices * 16)) * 16
    shape = (streams, devices, unit, chans)
    plans = stream_plans(clip_size, tm_size, streams)
    exchanges = max(sum((1 << len(weights)) - 1 for _, weights in plan) for plan in plans)
    flat = (frames * pixels, chans)
    hbm = pl.BlockSpec(memory_space=pltpu.HBM)
    vmem = pl.BlockSpec(memory_space=pltpu.VMEM)
    dma = pltpu.SemaphoreType.DMA
    mixed, total = pl.pallas_call(
        functools.partial(block_kernel, plans, tm_size),
        out_shape=(
            jax.ShapeDtypeStruct(flat, BF16),
            jax.ShapeDtypeStruct(shape, BF16),
        ),
        in_specs=[hbm] * 6,
        out_specs=(vmem, vmem),
        scratch_shapes=[
            pltpu.VMEM((frames, height, width, in_chans), BF16),
            pltpu.VMEM((4, LEAD + width, in_chans), F32),
            pltpu.VMEM((frames, rows, cols, taps), BF16),
            pltpu.VMEM((frames, rows + 1, cols, taps), BF16),
            pltpu.VMEM((frames, taps, pixels), BF16),
            pltpu.VMEM((frames, taps, pixels), BF16),
            pltpu.VMEM(flat, F32),
            pltpu.VMEM(flat, F32),
            pltpu.VMEM(flat, BF16),
            pltpu.VMEM((frames, chans, pixels), BF16),
        ]
        + [pltpu.VMEM(flat, BF16)] * 5
        + [
            pltpu.VMEM((pixels, chans), F32),
            pltpu.VMEM((pixels + cols, chans), BF16),
            pltpu.VMEM(flat, F32),
            pltpu.VMEM((3 * taps, chans), BF16),
            pltpu.VMEM((3, chans, chans), BF16),
            pltpu.VMEM((1, chans), F32),
            pltpu.VMEM((1, chans), F32),
            pltpu.VMEM(shape, F32),
            pltpu.VMEM(shape, BF16),
            pltpu.VMEM(shape, BF16),
            dma((frames + 5,)),
            dma((4, CHUNKS * PARTS)),
            dma((4, CHUNKS * PARTS)),
        ]
        + [dma((streams, exchanges))] * 4
        + [pltpu.SemaphoreType.REGULAR((2,))],
        compiler_params=pltpu.CompilerParams(
            collective_id=0, has_side_effects=True, vmem_limit_bytes=44 * 1024 * 1024
        ),
    )(
        in_hbm(clip_frames[0]),
        in_hbm(spatial_weight.reshape(3 * taps, chans)),
        in_hbm(norm_gain[None]),
        in_hbm(norm_bias[None]),
        in_hbm(temporal_weight),
        in_hbm(cotangent.reshape(flat)),
    )
    spatial_rows, temporal_rows = 3 * taps, 3 * chans
    mixed, spatial, temporal, gain, bias = pl.pallas_call(
        functools.partial(finish_kernel, spatial_rows),
        out_shape=(
            jax.ShapeDtypeStruct(flat, BF16),
            jax.ShapeDtypeStruct((spatial_rows, chans), F32),
            jax.ShapeDtypeStruct((temporal_rows, chans), F32),
            jax.ShapeDtypeStruct((1, chans), F32),
            jax.ShapeDtypeStruct((1, chans), F32),
        ),
        in_specs=[vmem, vmem],
        out_specs=(hbm, hbm, hbm, vmem, vmem),
        scratch_shapes=[pltpu.VMEM((spatial_rows + temporal_rows, chans), F32), dma((7,))],
        compiler_params=pltpu.CompilerParams(vmem_limit_bytes=12 * 1024 * 1024),
    )(total, mixed)
    return (
        mixed.reshape(cotangent.shape),
        spatial.reshape(spatial_weight.shape),
        gain[0],
        bias[0],
        temporal.reshape(temporal_weight.shape),
    )


def solution(mesh):
    return jax.shard_map(
        functools.partial(per_device, mesh.shape["clip"], mesh.shape["tm"]),
        mesh=mesh,
        in_specs=(
            P("clip", "tm", None, None, None),
            P(),
            P(),
            P(),
            P(),
            P("clip", "tm", None, None, None),
        ),
        out_specs=(P("clip", "tm", None, None, None), P(), P(), P(), P()),
        check_vma=False,
    )
```
